256 devices in a mesh: video: 4 (over z_hi, core), span: 16 (over y, z_lo), head: 4 (over x).
Axes of the slice: x: 4, y: 4, z: 8 (z_hi: 2, z_lo: 4; z = z_hi * 4 + z_lo), core: 2. Of those that a mesh axis runs over, the one named last changes fastest.
Arguments:
- queries: bfloat16 [16384, 48, 128], P(('video', 'span', 'head')), parts along dimension 0, may hold values from -15 to 15
- key_rows: bfloat16 [16384, 48, 128], P(('video', 'span', 'head')), parts along dimension 0, may hold values from -6 to 6
- value_rows: bfloat16 [16384, 48, 128], P(('video', 'span', 'head')), parts along dimension 0, may hold values from -6 to 6
- noise_levels: int32 [64], P('video'), parts along dimension 0, may hold values from 0 to 7
- gate_table: float32 [8, 48], replicated, may hold values from 0.25 to 2
Outputs:
- attended: bfloat16 [16384, 48, 128], P(('video', 'span', 'head')), parts along dimension 0
The draws below stay inside these ranges and needn't reach their ends.
There are 4 independent parts, one for each index of `video`. The reference program is written for one: setup_inputs(seed, part) draws one part's arguments, and reference() takes and returns one part's arrays. A program takes and returns all parts, laid end to end along the dimension named above; an argument that names none is the same for every part. Nothing has to cross between parts.
All inputs are finite; a program needn't handle non-finite values.
Results may differ from the reference program's by a relative error of at most 0.0039.
Values may be sent and summed in bfloat16 or wider, within the bound.
A program may use at most 128 MiB of HBM per device.

```python
import math
import jax
import jax.numpy as jnp
from jax import lax

HEADS = 48
HEAD_DIM = 128
BLOCK = 128
LEVELS = 8
CTOK = 256
SPANS = 16
TOKENS = 4096
N_SPAN = 16


def draw_queries(key, part):
    noise_field = 2.5 * jax.random.truncated_normal(jax.random.fold_in(key, 1), -6.0, 6.0, (TOKENS, HEADS, HEAD_DIM), jnp.float32)
    return noise_field.astype(jnp.bfloat16)


def draw_key_rows(key, part):
    noise_field = jax.random.truncated_normal(jax.random.fold_in(key, 2), -6.0, 6.0, (TOKENS, HEADS, HEAD_DIM), jnp.float32)
    return noise_field.astype(jnp.bfloat16)


def plant(array, own_key, low, largest):
    dims = array.shape
    index_at = [jax.random.randint(jax.random.fold_in(own_key, axis), (), 0, dims[axis]) for axis in range(len(dims))]
    array = array.at[tuple(index_at)].set(low)
    longest = dims.index(max(dims))
    index_at[longest] = (index_at[longest] + 1) % dims[longest]
    return array.at[tuple(index_at)].set(largest)


def levels(own_key, extent, shards, least, top_value):
    gain = 1.0
    for axis_at, parts in shards:
        steps = jax.random.uniform(jax.random.fold_in(jax.random.fold_in(own_key, 6), axis_at), (parts,), jnp.float32, least / len(shards), top_value / len(shards))
        gain = gain * jnp.repeat(jnp.exp(steps), extent[axis_at] // parts).reshape((-1,) + (1,) * (len(extent) - 1 - axis_at))
    return gain


def scatter_about(own_key, extent, scale, bound, cuts=(), kind=jnp.bfloat16):
    gain = levels(own_key, extent, cuts, -0.22, 0.18) if cuts else 1.0
    values = jax.random.normal(own_key, extent, jnp.float32) * scale * gain
    return jnp.minimum(jnp.maximum(values, -bound), bound).astype(kind)


def setup_inputs(seed: int = 0, part: int = 0) -> dict:
    seeds = jax.random.split(jax.random.key(seed), 6)
    part_keys = jax.random.split(jax.random.fold_in(seeds[5], part), 6)
    return {
        "queries": draw_queries(jax.random.fold_in(jax.random.fold_in(seeds[5], part), 71), part),
        "key_rows": draw_key_rows(jax.random.fold_in(jax.random.fold_in(seeds[5], part), 71), part),
        "value_rows": scatter_about(part_keys[2], (TOKENS, HEADS, HEAD_DIM), 1.0, 6.0, ((0, 64),)),
        "noise_levels": plant(jax.random.randint(part_keys[3], (SPANS,), 0, LEVELS), jax.random.fold_in(part_keys[3], 1), 0, LEVELS - 1).astype(jnp.int32),
        "gate_table": jnp.clip(jax.random.uniform(seeds[4], (LEVELS, HEADS), jnp.float32, 0.25, 2.0), 0.25, 2.0),
    }


def reference(queries, key_rows, value_rows, noise_levels, gate_table):
    score_scale = 1.0 / math.sqrt(HEAD_DIM)
    key_float = key_rows.astype(jnp.float32)
    value_float = value_rows.astype(jnp.float32)
    key_index = jnp.arange(TOKENS, dtype=jnp.int32)
    key_span = key_index // CTOK
    key_block = key_index % CTOK // BLOCK
    query_block = jnp.arange(CTOK, dtype=jnp.int32) // BLOCK

    def one_span(span_pos):
        first_row = (span_pos * CTOK).astype(jnp.int32)
        query_part = lax.dynamic_slice_in_dim(queries, first_row, CTOK, 0).astype(jnp.float32)
        scores = jnp.einsum('qhd,khd->qhk', query_part, key_float) * score_scale
        visible = (key_span[None, :] < span_pos) | (key_span[None, :] == span_pos) & (key_block[None, :] <= query_block[:, None])
        visible = visible[:, None, :]
        masked = jnp.where(visible, scores, -jnp.inf)
        row_max = lax.optimization_barrier(jnp.max(masked, axis=-1, keepdims=True))
        weights = jnp.where(visible, jnp.exp(masked - row_max), 0.0)
        totals = lax.optimization_barrier(jnp.sum(weights, axis=-1))
        rounded = lax.optimization_barrier(weights.astype(jnp.bfloat16))
        numerator = jnp.einsum('qhk,khd->qhd', rounded.astype(jnp.float32), value_float)
        one_hot = (jnp.arange(LEVELS, dtype=jnp.int32) == noise_levels[span_pos]).astype(jnp.float32)
        gate_row = jnp.dot(one_hot, gate_table, precision=lax.Precision.HIGHEST)
        result = numerator / totals[..., None] * gate_row[None, :, None]
        return result.astype(jnp.bfloat16)
    stacked = lax.map(one_span, jnp.arange(N_SPAN, dtype=jnp.int32))
    return stacked.reshape(TOKENS, HEADS, HEAD_DIM)
```

```python
import functools
import math

import jax
import jax.numpy as jnp
from jax import lax
from jax.experimental import pallas as pl
from jax.experimental.pallas import tpu as pltpu
from jax.sharding import PartitionSpec as P

MESH = pl.DeviceIdType.MESH
HEADS = 48
DIM = 128
ROWS = 64
SPANS = 16
QUARTERS = 4
SPAN = ROWS * QUARTERS
PEERS = SPANS * QUARTERS
GROUP = 4
CHUNK = SPAN * GROUP
CHUNKS = SPANS // GROUP
BLOCK = 128
HIDDEN = -1e30
SCALE = math.log2(math.e) / math.sqrt(DIM)


def pair_index(span, chunk):
    group = span // GROUP
    return 2 * group * (group + 1) + (span % GROUP) * (group + 1) + chunk


PAIRS = 2 * CHUNKS * (CHUNKS + 1)


def kernel(
    queries, key_rows, value_rows, noise_levels, gate_table, out,
    wide, send_qk, send_v, got_qk, got_v, scores, weights, totals, send_o, got_o,
    qk_sent, qk_here, v_sent, v_here, o_sent, o_here, own_qk, own_v,
):
    core = lax.axis_index("video") % 2
    span = lax.axis_index("span")
    x = lax.axis_index("head")
    y = span // 4
    z = span % 4
    me = span * QUARTERS + x

    def place(column_x, column_y, j):
        z_at = (0, 1 + core, 3)[j]
        return (column_y * 4 + column_x) * 3 + j, column_y * 4 + z_at, column_x

    active = (z == 0) | (z == 3) | (z == 1 + core)
    j_mine = jnp.where(z == 0, 0, jnp.where(z == 3, 2, 1))
    my_head = (y * 4 + x) * 3 + j_mine

    barrier = pltpu.get_barrier_semaphore()

    def greet(i, carry):
        other = lax.rem(me + i, PEERS)
        pl.semaphore_signal(
            barrier,
            inc=1,
            device_id={"span": other // QUARTERS, "head": other % QUARTERS},
            device_id_type=MESH,
        )
        return carry

    lax.fori_loop(1, PEERS, greet, 0)

    def by_head(ref, store):
        wide[...] = ref[...].reshape(ROWS * HEADS, DIM).astype(jnp.float32)

        def one(h, carry):
            store(h, wide[pl.ds(h, ROWS, stride=HEADS), :].astype(jnp.bfloat16))
            return carry

        lax.fori_loop(0, HEADS, one, 0)

    def store_q(h, rows):
        send_qk[h, 0] = rows

    def store_k(h, rows):
        send_qk[h, 1] = rows

    def store_v(h, rows):
        send_v[h] = rows

    by_head(queries, store_q)
    by_head(key_rows, store_k)
    pl.semaphore_wait(barrier, PEERS - 1)

    def scatter(source, target, sent, here, own):
        def column(k, carry):
            column_x = lax.rem(x + k % 4, 4)
            column_y = lax.rem(y + k // 4, 4)
            for j in range(3):
                head, to_span, to_x = place(column_x, column_y, j)
                mine = (to_span == span) & (to_x == x)

                @pl.when(jnp.logical_not(mine))
                def _():
                    pltpu.make_async_remote_copy(
                        source.at[head],
                        target.at[me],
                        sent,
                        here,
                        device_id={"span": to_span, "head": to_x},
                        device_id_type=MESH,
                    ).start()

                @pl.when(mine)
                def _():
                    pltpu.make_async_copy(source.at[head], target.at[me], own).start()

            return carry

        lax.fori_loop(0, 16, column, 0)

    scatter(send_qk, got_qk, qk_sent, qk_here, own_qk)
    by_head(value_rows, store_v)
    scatter(send_v, got_v, v_sent, v_here, own_v)

    def wait_for(ref, count, semaphore):
        part = ref.at[pl.ds(0, count)]
        pltpu.make_async_copy(part, part, semaphore).wait()

    @pl.when(active)
    def _():
        wait_for(got_qk, PEERS - 1, qk_here)
        wait_for(got_qk, 1, own_qk)

        def soften(i, carry):
            group = i // GROUP
            place_in_group = i % GROUP
            q = got_qk[pl.ds(i * QUARTERS, QUARTERS), 0].reshape(SPAN, DIM)

            def raw(c):
                keys = got_qk[pl.ds(c * (GROUP * QUARTERS), GROUP * QUARTERS), 1]
                return lax.dot_general(
                    q,
                    keys.reshape(CHUNK, DIM),
                    (((1,), (1,)), ((), ())),
                    preferred_element_type=jnp.float32,
                )

            def lanes(value, op):
                parts = [value[:, k * BLOCK : (k + 1) * BLOCK] for k in range(CHUNK // BLOCK)]
                while len(parts) > 1:
                    parts = [op(a, b) for a, b in zip(parts[::2], parts[1::2])]
                return parts[0]

            s = raw(group)
            columns = []
            for k in range(CHUNK // BLOCK):
                halves = []
                for half in range(SPAN // BLOCK):
                    block = s[half * BLOCK : (half + 1) * BLOCK, k * BLOCK : (k + 1) * BLOCK]
                    seen = k <= 2 * place_in_group + half
                    halves.append(jnp.where(seen, block, HIDDEN))
                columns.append(jnp.concatenate(halves, axis=0))
            s = jnp.concatenate(columns, axis=1)
            scores[group] = s
            top = lanes(s, jnp.maximum)

            def full(c, top):
                s = raw(c)
                scores[c] = s
                return jnp.maximum(top, lanes(s, jnp.maximum))

            top = lax.fori_loop(0, group, full, top)
            row_max = jnp.max(top, axis=1, keepdims=True)

            def weigh(c, total):
                w = jnp.exp2((scores[c] - row_max) * SCALE)
                weights[pair_index(i, c)] = w.astype(jnp.bfloat16)
                return total + lanes(w, jnp.add)

            total = lax.fori_loop(0, group + 1, weigh, jnp.zeros((SPAN, BLOCK), jnp.float32))
            totals[i] = jnp.sum(total, axis=1, keepdims=True)
            return carry

        lax.fori_loop(0, SPANS, soften, 0)

        wait_for(got_v, PEERS - 1, v_here)
        wait_for(got_v, 1, own_v)

        def gather(i, carry):
            def add(c, acc):
                values = got_v[pl.ds(c * (GROUP * QUARTERS), GROUP * QUARTERS)]
                return acc + jnp.dot(
                    weights[pair_index(i, c)],
                    values.reshape(CHUNK, DIM),
                    preferred_element_type=jnp.float32,
                )

            acc = lax.fori_loop(0, i // GROUP + 1, add, jnp.zeros((SPAN, DIM), jnp.float32))
            gate = gate_table[noise_levels[i], my_head]
            result = (acc / totals[i] * gate).astype(jnp.bfloat16)
            send_o[pl.ds(i * QUARTERS, QUARTERS)] = result.reshape(QUARTERS, ROWS, DIM)
            for quarter in range(QUARTERS):
                piece = i * QUARTERS + quarter
                mine = piece == me

                @pl.when(jnp.logical_not(mine))
                def _():
                    pltpu.make_async_remote_copy(
                        send_o.at[piece],
                        got_o.at[my_head],
                        o_sent,
                        o_here,
                        device_id={"span": i, "head": quarter},
                        device_id_type=MESH,
                    ).start()

                @pl.when(mine)
                def _():
                    got_o[my_head] = send_o[piece]

            return carry

        lax.fori_loop(0, SPANS, gather, 0)
        wait_for(got_o, HEADS - 1, o_here)
        wait_for(send_qk, HEADS - 1, qk_sent)
        wait_for(send_v, HEADS - 1, v_sent)
        wait_for(send_o, PEERS - 1, o_sent)

    @pl.when(jnp.logical_not(active))
    def _():
        wait_for(got_o, HEADS, o_here)
        wait_for(send_qk, HEADS, qk_sent)
        wait_for(send_v, HEADS, v_sent)

    wide[...] = got_o[...].reshape(HEADS * ROWS, DIM).astype(jnp.float32)

    def token(t, carry):
        out[t] = wide[pl.ds(t, HEADS, stride=ROWS), :].astype(jnp.bfloat16)
        return carry

    lax.fori_loop(0, ROWS, token, 0)


def body(queries, key_rows, value_rows, noise_levels, gate_table):
    vmem = pl.BlockSpec(memory_space=pltpu.VMEM)
    smem = pl.BlockSpec(memory_space=pltpu.SMEM)
    bf16, f32 = jnp.bfloat16, jnp.float32
    return pl.pallas_call(
        kernel,
        out_shape=jax.ShapeDtypeStruct((ROWS, HEADS, DIM), bf16),
        in_specs=[vmem, vmem, vmem, smem, smem],
        out_specs=vmem,
        scratch_shapes=[
            pltpu.VMEM((ROWS * HEADS, DIM), f32),
            pltpu.VMEM((HEADS, 2, ROWS, DIM), bf16),
            pltpu.VMEM((HEADS, ROWS, DIM), bf16),
            pltpu.VMEM((PEERS, 2, ROWS, DIM), bf16),
            pltpu.VMEM((PEERS, ROWS, DIM), bf16),
            pltpu.VMEM((CHUNKS, SPAN, CHUNK), f32),
            pltpu.VMEM((PAIRS, SPAN, CHUNK), bf16),
            pltpu.VMEM((SPANS, SPAN, 1), f32),
            pltpu.VMEM((PEERS, ROWS, DIM), bf16),
            pltpu.VMEM((HEADS, ROWS, DIM), bf16),
        ]
        + [pltpu.SemaphoreType.DMA] * 8,
        compiler_params=pltpu.CompilerParams(
            collective_id=0, has_side_effects=True, vmem_limit_bytes=56 << 20
        ),
    )(queries, key_rows, value_rows, noise_levels, gate_table)


def solution(mesh):
    return jax.shard_map(
        body,
        mesh=mesh,
        in_specs=(
            P(("video", "span", "head"), None, None),
            P(("video", "span", "head"), None, None),
            P(("video", "span", "head"), None, None),
            P("video"),
            P(),
        ),
        out_specs=P(("video", "span", "head"), None, None),
        check_vma=False,
    )
```

```python
import functools
import math

import jax
import jax.numpy as jnp
from jax import lax
from jax.experimental import pallas as pl
from jax.experimental.pallas import tpu as pltpu
from jax.sharding import PartitionSpec as P

MESH = pl.DeviceIdType.MESH
HEADS = 48
DIM = 128
ROWS = 64
SPANS = 16
QUARTERS = 4
SPAN = ROWS * QUARTERS
PEERS = SPANS * QUARTERS
GROUP = 4
CHUNK = SPAN * GROUP
CHUNKS = SPANS // GROUP
BLOCK = 128
HIDDEN = -1e30
SCALE = math.log2(math.e) / math.sqrt(DIM)
PAIRS = CHUNKS * (CHUNKS + 1) // 2


def pair_at(group, chunk):
    return group * (group + 1) // 2 + chunk


def raw_scores(q, keys):
    return lax.dot_general(q, keys, (((1,), (1,)), ((), ())), preferred_element_type=jnp.float32)


def blocks_of(value):
    return [value[:, k * BLOCK : (k + 1) * BLOCK] for k in range(value.shape[1] // BLOCK)]


def fold(parts, op):
    parts = list(parts)
    while len(parts) > 1:
        paired = [op(left, right) for left, right in zip(parts[::2], parts[1::2])]
        parts = paired + (parts[-1:] if len(parts) % 2 else [])
    return parts[0]


def kernel(
    queries, key_rows, value_rows, noise_levels, gate_table, out,
    wide, send_qk, send_v, got_qk, got_v, weights, peaks, tops, shares, sums, acc, send_o, got_o,
    qk_sent, qk_here, v_sent, v_here, o_sent, o_here, own_qk, own_v,
):
    core = lax.axis_index("video") % 2
    span = lax.axis_index("span")
    x = lax.axis_index("head")
    y = span // 4
    z = span % 4
    me = span * QUARTERS + x

    def place(column_x, column_y, j):
        z_at = (0, 1 + core, 3)[j]
        return (column_y * 4 + column_x) * 3 + j, column_y * 4 + z_at, column_x

    active = (z == 0) | (z == 3) | (z == 1 + core)
    j_mine = jnp.where(z == 0, 0, jnp.where(z == 3, 2, 1))
    my_head = (y * 4 + x) * 3 + j_mine

    barrier = pltpu.get_barrier_semaphore()

    def greet(i, carry):
        other = lax.rem(me + i, PEERS)
        pl.semaphore_signal(
            barrier,
            inc=1,
            device_id={"span": other // QUARTERS, "head": other % QUARTERS},
            device_id_type=MESH,
        )
        return carry

    lax.fori_loop(1, PEERS, greet, 0)

    def by_head(ref, store):
        wide[...] = ref[...].reshape(ROWS * HEADS, DIM).astype(jnp.float32)

        def one(h, carry):
            store(h, wide[pl.ds(h, ROWS, stride=HEADS), :].astype(jnp.bfloat16))
            return carry

        lax.fori_loop(0, HEADS, one, 0)

    def store_q(h, rows):
        send_qk[h, 0] = rows

    def store_k(h, rows):
        send_qk[h, 1] = rows

    def store_v(h, rows):
        send_v[h] = rows

    by_head(queries, store_q)
    by_head(key_rows, store_k)
    pl.semaphore_wait(barrier, PEERS - 1)

    def scatter(source, target, sent, here, own):
        def column(k, carry):
            column_x = lax.rem(x + k % 4, 4)
            column_y = lax.rem(y + k // 4, 4)
            for j in range(3):
                head, to_span, to_x = place(column_x, column_y, j)
                mine = (to_span == span) & (to_x == x)

                @pl.when(jnp.logical_not(mine))
                def _():
                    pltpu.make_async_remote_copy(
                        source.at[head],
                        target.at[me],
                        sent,
                        here,
                        device_id={"span": to_span, "head": to_x},
                        device_id_type=MESH,
                    ).start()

                @pl.when(mine)
                def _():
                    pltpu.make_async_copy(source.at[head], target.at[me], own).start()

            return carry

        lax.fori_loop(0, 16, column, 0)

    scatter(send_qk, got_qk, qk_sent, qk_here, own_qk)
    by_head(value_rows, store_v)
    scatter(send_v, got_v, v_sent, v_here, own_v)

    def wait_for(ref, count, semaphore):
        part = ref.at[pl.ds(0, count)]
        pltpu.make_async_copy(part, part, semaphore).wait()

    @pl.when(active)
    def _():
        wait_for(got_qk, PEERS - 1, qk_here)
        wait_for(got_qk, 1, own_qk)

        def q_of(group, r):
            return got_qk[pl.ds((group * GROUP + r) * QUARTERS, QUARTERS), 0].reshape(SPAN, DIM)

        def keys_of(chunk, spans):
            first = chunk * (GROUP * QUARTERS)
            return got_qk[pl.ds(first, spans * QUARTERS), 1].reshape(spans * SPAN, DIM)

        def values_of(chunk, spans):
            first = chunk * (GROUP * QUARTERS)
            return got_v[pl.ds(first, spans * QUARTERS)].reshape(spans * SPAN, DIM)

        def weigh(pair, r, columns, top):
            ws = [jnp.exp2((s - top) * SCALE) for s in columns]
            for k, w in enumerate(ws):
                weights[pair, r, :, k * BLOCK : (k + 1) * BLOCK] = w.astype(jnp.bfloat16)
            peaks[pair, r] = top
            return fold(ws, jnp.add)

        def soften(group, carry):
            for r in range(GROUP):
                columns = blocks_of(raw_scores(q_of(group, r), keys_of(group, r + 1)))
                hidden = jnp.full((BLOCK, BLOCK), HIDDEN, jnp.float32)
                columns[-1] = jnp.concatenate([hidden, columns[-1][BLOCK:]], axis=0)
                top = jnp.max(fold(columns, jnp.maximum), axis=1, keepdims=True)
                sums[r] = weigh(pair_at(group, group), r, columns, top)
                tops[group, r] = top

            def earlier(chunk, carry):
                for r in range(GROUP):
                    columns = blocks_of(raw_scores(q_of(group, r), keys_of(chunk, GROUP)))
                    before = tops[group, r]
                    top = jnp.max(fold(columns, jnp.maximum), axis=1, keepdims=True)
                    top = jnp.maximum(before, top)
                    added = weigh(pair_at(group, chunk), r, columns, top)
                    sums[r] = sums[r] * jnp.exp2((before - top) * SCALE) + added
                    tops[group, r] = top
                return carry

            lax.fori_loop(0, group, earlier, 0)
            for r in range(GROUP):
                gate = gate_table[noise_levels[group * GROUP + r], my_head]
                shares[group, r] = gate / jnp.sum(sums[r], axis=1, keepdims=True)
            return carry

        lax.fori_loop(0, CHUNKS, soften, 0)

        wait_for(got_v, PEERS - 1, v_here)
        wait_for(got_v, 1, own_v)

        def gather(step, carry):
            group = step

            def term(chunk, spans, r):
                pair = pair_at(group, chunk)
                rescale = jnp.exp2((peaks[pair, r] - tops[group, r]) * SCALE)
                return rescale * jnp.dot(
                    weights[pair, r, :, 0 : spans * SPAN],
                    values_of(chunk, spans),
                    preferred_element_type=jnp.float32,
                )

            for r in range(GROUP):
                acc[r] = term(group, r + 1, r)

            def earlier(chunk, carry):
                for r in range(GROUP):
                    acc[r] += term(chunk, GROUP, r)
                return carry

            lax.fori_loop(0, group, earlier, 0)
            for r in range(GROUP):
                i = group * GROUP + r
                result = (acc[r] * shares[group, r]).astype(jnp.bfloat16)
                send_o[pl.ds(i * QUARTERS, QUARTERS)] = result.reshape(QUARTERS, ROWS, DIM)
                for quarter in range(QUARTERS):
                    piece = i * QUARTERS + quarter
                    mine = piece == me

                    @pl.when(jnp.logical_not(mine))
                    def _():
                        pltpu.make_async_remote_copy(
                            send_o.at[piece],
                            got_o.at[my_head],
                            o_sent,
                            o_here,
                            device_id={"span": i, "head": quarter},
                            device_id_type=MESH,
                        ).start()

                    @pl.when(mine)
                    def _():
                        got_o[my_head] = send_o[piece]

            return carry

        lax.fori_loop(0, CHUNKS, gather, 0)
        wait_for(got_o, HEADS - 1, o_here)
        wait_for(send_qk, HEADS - 1, qk_sent)
        wait_for(send_v, HEADS - 1, v_sent)
        wait_for(send_o, PEERS - 1, o_sent)

    @pl.when(jnp.logical_not(active))
    def _():
        wait_for(got_o, HEADS, o_here)
        wait_for(send_qk, HEADS, qk_sent)
        wait_for(send_v, HEADS, v_sent)

    wide[...] = got_o[...].reshape(HEADS * ROWS, DIM).astype(jnp.float32)

    def token(t, carry):
        out[t] = wide[pl.ds(t, HEADS, stride=ROWS), :].astype(jnp.bfloat16)
        return carry

    lax.fori_loop(0, ROWS, token, 0)


def body(queries, key_rows, value_rows, noise_levels, gate_table):
    vmem = pl.BlockSpec(memory_space=pltpu.VMEM)
    smem = pl.BlockSpec(memory_space=pltpu.SMEM)
    bf16, f32 = jnp.bfloat16, jnp.float32
    return pl.pallas_call(
        kernel,
        out_shape=jax.ShapeDtypeStruct((ROWS, HEADS, DIM), bf16),
        in_specs=[vmem, vmem, vmem, smem, smem],
        out_specs=vmem,
        scratch_shapes=[
            pltpu.VMEM((ROWS * HEADS, DIM), f32),
            pltpu.VMEM((HEADS, 2, ROWS, DIM), bf16),
            pltpu.VMEM((HEADS, ROWS, DIM), bf16),
            pltpu.VMEM((PEERS, 2, ROWS, DIM), bf16),
            pltpu.VMEM((PEERS, ROWS, DIM), bf16),
            pltpu.VMEM((PAIRS, GROUP, SPAN, CHUNK), bf16),
            pltpu.VMEM((PAIRS, GROUP, SPAN, 1), f32),
            pltpu.VMEM((CHUNKS, GROUP, SPAN, 1), f32),
            pltpu.VMEM((CHUNKS, GROUP, SPAN, 1), f32),
            pltpu.VMEM((GROUP, SPAN, BLOCK), f32),
            pltpu.VMEM((GROUP, SPAN, DIM), f32),
            pltpu.VMEM((PEERS, ROWS, DIM), bf16),
            pltpu.VMEM((HEADS, ROWS, DIM), bf16),
        ]
        + [pltpu.SemaphoreType.DMA] * 8,
        compiler_params=pltpu.CompilerParams(
            collective_id=0, has_side_effects=True, vmem_limit_bytes=56 << 20
        ),
    )(queries, key_rows, value_rows, noise_levels, gate_table)


def solution(mesh):
    return jax.shard_map(
        body,
        mesh=mesh,
        in_specs=(
            P(("video", "span", "head"), None, None),
            P(("video", "span", "head"), None, None),
            P(("video", "span", "head"), None, None),
            P("video"),
            P(),
        ),
        out_specs=P(("video", "span", "head"), None, None),
        check_vma=False,
    )
```

```python
import functools
import math

import jax
import jax.numpy as jnp
from jax import lax
from jax.experimental import pallas as pl
from jax.experimental.pallas import tpu as pltpu
from jax.sharding import PartitionSpec as P

MESH = pl.DeviceIdType.MESH
HEADS = 48
DIM = 128
ROWS = 64
SPANS = 16
QUARTERS = 4
SPAN = ROWS * QUARTERS
PEERS = SPANS * QUARTERS
GROUP = 4
CHUNK = SPAN * GROUP
CHUNKS = SPANS // GROUP
BLOCK = 128
HIDDEN = -1e30
SCALE = math.log2(math.e) / math.sqrt(DIM)
PAIRS = CHUNKS * (CHUNKS + 1) // 2


def pair_at(group, chunk):
    return group * (group + 1) // 2 + chunk


def raw_scores(q, keys):
    return lax.dot_general(q, keys, (((1,), (1,)), ((), ())), preferred_element_type=jnp.float32)


def blocks_of(value):
    return [value[:, k * BLOCK : (k + 1) * BLOCK] for k in range(value.shape[1] // BLOCK)]


def fold(parts, op):
    parts = list(parts)
    while len(parts) > 1:
        paired = [op(left, right) for left, right in zip(parts[::2], parts[1::2])]
        parts = paired + (parts[-1:] if len(parts) % 2 else [])
    return parts[0]


def kernel(
    queries_hbm, key_rows_hbm, value_rows_hbm, noise_levels, gate_table, out,
    queries, key_rows, value_rows, loaded, wide, send_qk, send_v, got_qk, got_v, weights, peaks, tops, shares, sums, acc, send_o, got_o,
    qk_sent, qk_here, v_sent, v_here, o_sent, o_here, own_qk, own_v, plane_in,
):
    core = lax.axis_index("video") % 2
    span = lax.axis_index("span")
    x = lax.axis_index("head")
    y = span // 4
    z = span % 4
    me = span * QUARTERS + x

    def place(column_x, column_y, j):
        z_at = (0, 1 + core, 3)[j]
        return (column_y * 4 + column_x) * 3 + j, column_y * 4 + z_at, column_x

    active = (z == 0) | (z == 3) | (z == 1 + core)
    j_mine = jnp.where(z == 0, 0, jnp.where(z == 3, 2, 1))
    my_head = (y * 4 + x) * 3 + j_mine

    loads = [
        pltpu.make_async_copy(source, target, loaded.at[n])
        for n, (source, target) in enumerate(
            [(queries_hbm, queries), (key_rows_hbm, key_rows), (value_rows_hbm, value_rows)]
        )
    ]
    for load in loads:
        load.start()

    barrier = pltpu.get_barrier_semaphore()

    def signal(semaphore, to_span, to_x):
        pl.semaphore_signal(
            semaphore,
            inc=1,
            device_id={"span": to_span, "head": to_x},
            device_id_type=MESH,
        )

    def greet_column(semaphore):
        for i in range(1, 4):
            signal(semaphore, y * 4 + lax.rem(z + i, 4), x)

    greet_column(barrier)
    for i in range(1, 16):
        signal(barrier, lax.rem(y + i // 4, 4) * 4 + z, lax.rem(x + i % 4, 4))

    def by_head(ref, store):
        wide[...] = ref[...].reshape(ROWS * HEADS, DIM).astype(jnp.float32)

        def one(h, carry):
            store(h, wide[pl.ds(h, ROWS, stride=HEADS), :].astype(jnp.bfloat16))
            return carry

        lax.fori_loop(0, HEADS, one, 0)

    def store_q(h, rows):
        send_qk[h, 0] = rows

    def store_k(h, rows):
        send_qk[h, 1] = rows

    def store_v(h, rows):
        send_v[h] = rows

    loads[0].wait()
    by_head(queries, store_q)
    loads[1].wait()
    by_head(key_rows, store_k)
    pl.semaphore_wait(barrier, 3 + 15)
    greet_column(plane_in)

    def scatter(first, last, source, target, sent, here, own):
        def column(k, carry):
            column_x = lax.rem(x + k % 4, 4)
            column_y = lax.rem(y + k // 4, 4)
            for j in range(3):
                head, to_span, to_x = place(column_x, column_y, j)
                mine = (to_span == span) & (to_x == x)

                @pl.when(jnp.logical_not(mine))
                def _():
                    pltpu.make_async_remote_copy(
                        source.at[head],
                        target.at[me],
                        sent,
                        here,
                        device_id={"span": to_span, "head": to_x},
                        device_id_type=MESH,
                    ).start()

                @pl.when(mine)
                def _():
                    pltpu.make_async_copy(source.at[head], target.at[me], own).start()

            return carry

        lax.fori_loop(first, last, column, 0)

    scatter(0, 1, send_qk, got_qk, qk_sent, qk_here.at[y], own_qk)
    pl.semaphore_wait(plane_in, 3)
    scatter(1, 16, send_qk, got_qk, qk_sent, qk_here.at[y], own_qk)
    loads[2].wait()
    by_head(value_rows, store_v)
    scatter(0, 16, send_v, got_v, v_sent, v_here, own_v)

    def wait_for(ref, count, semaphore):
        part = ref.at[pl.ds(0, count)]
        pltpu.make_async_copy(part, part, semaphore).wait()

    @pl.when(active)
    def _():
        def q_of(group, r):
            return got_qk[pl.ds((group * GROUP + r) * QUARTERS, QUARTERS), 0].reshape(SPAN, DIM)

        def keys_of(chunk, spans):
            first = chunk * (GROUP * QUARTERS)
            return got_qk[pl.ds(first, spans * QUARTERS), 1].reshape(spans * SPAN, DIM)

        def values_of(chunk, spans):
            first = chunk * (GROUP * QUARTERS)
            return got_v[pl.ds(first, spans * QUARTERS)].reshape(spans * SPAN, DIM)

        def weigh(pair, r, columns, top):
            ws = [jnp.exp2((s - top) * SCALE) for s in columns]
            for k, w in enumerate(ws):
                weights[pair, r, :, k * BLOCK : (k + 1) * BLOCK] = w.astype(jnp.bfloat16)
            peaks[pair, r] = top
            return fold(ws, jnp.add)

        def own_chunk(group):
            for r in range(GROUP):
                columns = blocks_of(raw_scores(q_of(group, r), keys_of(group, r + 1)))
                hidden = jnp.full((BLOCK, BLOCK), HIDDEN, jnp.float32)
                columns[-1] = jnp.concatenate([hidden, columns[-1][BLOCK:]], axis=0)
                top = jnp.max(fold(columns, jnp.maximum), axis=1, keepdims=True)
                sums[group, r] = weigh(pair_at(group, group), r, columns, top)
                tops[group, r] = top

        def earlier_chunk(group, chunk):
            for r in range(GROUP):
                columns = blocks_of(raw_scores(q_of(group, r), keys_of(chunk, GROUP)))
                before = tops[group, r]
                top = jnp.max(fold(columns, jnp.maximum), axis=1, keepdims=True)
                top = jnp.maximum(before, top)
                added = weigh(pair_at(group, chunk), r, columns, top)
                sums[group, r] = sums[group, r] * jnp.exp2((before - top) * SCALE) + added
                tops[group, r] = top

        def row_of(step):
            return lax.rem(y + CHUNKS - step, CHUNKS)

        def soften(step, carry):
            row = row_of(step)

            @pl.when(step == 0)
            def _():
                wait_for(got_qk, 15, qk_here.at[row])
                wait_for(got_qk, 1, own_qk)

            @pl.when(step > 0)
            def _():
                wait_for(got_qk, 16, qk_here.at[row])

            own_chunk(row)

            def with_row(before, carry):
                other = row_of(before)
                earlier_chunk(jnp.maximum(row, other), jnp.minimum(row, other))
                return carry

            lax.fori_loop(0, step, with_row, 0)
            return carry

        lax.fori_loop(0, CHUNKS, soften, 0)

        def share(group, carry):
            for r in range(GROUP):
                gate = gate_table[noise_levels[group * GROUP + r], my_head]
                shares[group, r] = gate / jnp.sum(sums[group, r], axis=1, keepdims=True)
            return carry

        lax.fori_loop(0, CHUNKS, share, 0)

        wait_for(got_v, PEERS - 1, v_here)
        wait_for(got_v, 1, own_v)

        def gather(step, carry):
            group = step

            def term(chunk, spans, r):
                pair = pair_at(group, chunk)
                rescale = jnp.exp2((peaks[pair, r] - tops[group, r]) * SCALE)
                return rescale * jnp.dot(
                    weights[pair, r, :, 0 : spans * SPAN],
                    values_of(chunk, spans),
                    preferred_element_type=jnp.float32,
                )

            for r in range(GROUP):
                acc[r] = term(group, r + 1, r)

            def earlier(chunk, carry):
                for r in range(GROUP):
                    acc[r] += term(chunk, GROUP, r)
                return carry

            lax.fori_loop(0, group, earlier, 0)
            for r in range(GROUP):
                i = group * GROUP + r
                result = (acc[r] * shares[group, r]).astype(jnp.bfloat16)
                send_o[pl.ds(i * QUARTERS, QUARTERS)] = result.reshape(QUARTERS, ROWS, DIM)
                for quarter in range(QUARTERS):
                    piece = i * QUARTERS + quarter
                    mine = piece == me

                    @pl.when(jnp.logical_not(mine))
                    def _():
                        pltpu.make_async_remote_copy(
                            send_o.at[piece],
                            got_o.at[my_head],
                            o_sent,
                            o_here,
                            device_id={"span": i, "head": quarter},
                            device_id_type=MESH,
                        ).start()

                    @pl.when(mine)
                    def _():
                        got_o[my_head] = send_o[piece]

            return carry

        lax.fori_loop(0, CHUNKS, gather, 0)
        wait_for(got_o, HEADS - 1, o_here)
        wait_for(send_qk, HEADS - 1, qk_sent)
        wait_for(send_v, HEADS - 1, v_sent)
        wait_for(send_o, PEERS - 1, o_sent)

    @pl.when(jnp.logical_not(active))
    def _():
        wait_for(got_o, HEADS, o_here)
        wait_for(send_qk, HEADS, qk_sent)
        wait_for(send_v, HEADS, v_sent)

    wide[...] = got_o[...].reshape(HEADS * ROWS, DIM).astype(jnp.float32)

    def token(t, carry):
        out[t] = wide[pl.ds(t, HEADS, stride=ROWS), :].astype(jnp.bfloat16)
        return carry

    lax.fori_loop(0, ROWS, token, 0)


def body(queries, key_rows, value_rows, noise_levels, gate_table):
    vmem = pl.BlockSpec(memory_space=pltpu.VMEM)
    smem = pl.BlockSpec(memory_space=pltpu.SMEM)
    hbm = pl.BlockSpec(memory_space=pl.ANY)
    dma = pltpu.SemaphoreType.DMA
    bf16, f32 = jnp.bfloat16, jnp.float32
    return pl.pallas_call(
        kernel,
        out_shape=jax.ShapeDtypeStruct((ROWS, HEADS, DIM), bf16),
        in_specs=[hbm, hbm, hbm, smem, smem],
        out_specs=vmem,
        scratch_shapes=[pltpu.VMEM((ROWS, HEADS, DIM), bf16)] * 3
        + [
            dma((3,)),
            pltpu.VMEM((ROWS * HEADS, DIM), f32),
            pltpu.VMEM((HEADS, 2, ROWS, DIM), bf16),
            pltpu.VMEM((HEADS, ROWS, DIM), bf16),
            pltpu.VMEM((PEERS, 2, ROWS, DIM), bf16),
            pltpu.VMEM((PEERS, ROWS, DIM), bf16),
            pltpu.VMEM((PAIRS, GROUP, SPAN, CHUNK), bf16),
            pltpu.VMEM((PAIRS, GROUP, SPAN, 1), f32),
            pltpu.VMEM((CHUNKS, GROUP, SPAN, 1), f32),
            pltpu.VMEM((CHUNKS, GROUP, SPAN, 1), f32),
            pltpu.VMEM((CHUNKS, GROUP, SPAN, BLOCK), f32),
            pltpu.VMEM((GROUP, SPAN, DIM), f32),
            pltpu.VMEM((PEERS, ROWS, DIM), bf16),
            pltpu.VMEM((HEADS, ROWS, DIM), bf16),
        ]
        + [dma, dma((CHUNKS,))] + [dma] * 6 + [pltpu.SemaphoreType.REGULAR],
        compiler_params=pltpu.CompilerParams(
            collective_id=0, has_side_effects=True, vmem_limit_bytes=56 << 20
        ),
    )(queries, key_rows, value_rows, noise_levels, gate_table)


def solution(mesh):
    return jax.shard_map(
        body,
        mesh=mesh,
        in_specs=(
            P(("video", "span", "head"), None, None),
            P(("video", "span", "head"), None, None),
            P(("video", "span", "head"), None, None),
            P("video"),
            P(),
        ),
        out_specs=P(("video", "span", "head"), None, None),
        check_vma=False,
    )
```

```python
import functools
import math

import jax
import jax.numpy as jnp
from jax import lax
from jax.experimental import pallas as pl
from jax.experimental.pallas import tpu as pltpu
from jax.sharding import PartitionSpec as P

MESH = pl.DeviceIdType.MESH
HEADS = 48
DIM = 128
ROWS = 64
SPANS = 16
QUARTERS = 4
SPAN = ROWS * QUARTERS
PEERS = SPANS * QUARTERS
GROUP = 4
CHUNK = SPAN * GROUP
CHUNKS = SPANS // GROUP
BLOCK = 128
HIDDEN = -1e30
SCALE = math.log2(math.e) / math.sqrt(DIM)
PAIRS = CHUNKS * (CHUNKS + 1) // 2


def pair_at(group, chunk):
    return group * (group + 1) // 2 + chunk


def raw_scores(q, keys):
    return lax.dot_general(q, keys, (((1,), (1,)), ((), ())), preferred_element_type=jnp.float32)


def blocks_of(value):
    return [value[:, k * BLOCK : (k + 1) * BLOCK] for k in range(value.shape[1] // BLOCK)]


def fold(parts, op):
    parts = list(parts)
    while len(parts) > 1:
        paired = [op(left, right) for left, right in zip(parts[::2], parts[1::2])]
        parts = paired + (parts[-1:] if len(parts) % 2 else [])
    return parts[0]


def kernel(
    queries_hbm, key_rows_hbm, value_rows_hbm, noise_levels, gate_table, got_o,
    queries, key_rows, value_rows, loaded, wide, send_qk, send_v, got_qk, got_v, weights, peaks, tops, shares, sums, acc, send_o,
    qk_sent, qk_here, v_sent, v_here, o_sent, o_here, own_qk, own_v, own_o, plane_in,
):
    core = lax.axis_index("video") % 2
    span = lax.axis_index("span")
    x = lax.axis_index("head")
    y = span // 4
    z = span % 4
    me = span * QUARTERS + x

    def place(column_x, column_y, j):
        z_at = (0, 1 + core, 3)[j]
        return (column_y * 4 + column_x) * 3 + j, column_y * 4 + z_at, column_x

    active = (z == 0) | (z == 3) | (z == 1 + core)
    j_mine = jnp.where(z == 0, 0, jnp.where(z == 3, 2, 1))
    my_head = (y * 4 + x) * 3 + j_mine

    loads = [
        pltpu.make_async_copy(source, target, loaded.at[n])
        for n, (source, target) in enumerate(
            [(queries_hbm, queries), (key_rows_hbm, key_rows), (value_rows_hbm, value_rows)]
        )
    ]
    for load in loads:
        load.start()

    barrier = pltpu.get_barrier_semaphore()

    def signal(semaphore, to_span, to_x):
        pl.semaphore_signal(
            semaphore,
            inc=1,
            device_id={"span": to_span, "head": to_x},
            device_id_type=MESH,
        )

    def greet_column(semaphore):
        for i in range(1, 4):
            signal(semaphore, y * 4 + lax.rem(z + i, 4), x)

    greet_column(barrier)
    for i in range(1, 16):
        signal(barrier, lax.rem(y + i // 4, 4) * 4 + z, lax.rem(x + i % 4, 4))

    def by_head(ref, store):
        wide[...] = ref[...].reshape(ROWS * HEADS, DIM).astype(jnp.float32)

        def one(h, carry):
            store(h, wide[pl.ds(h, ROWS, stride=HEADS), :].astype(jnp.bfloat16))
            return carry

        lax.fori_loop(0, HEADS, one, 0)

    def store_q(h, rows):
        send_qk[h, 0] = rows

    def store_k(h, rows):
        send_qk[h, 1] = rows

    def store_v(h, rows):
        send_v[h] = rows

    loads[0].wait()
    by_head(queries, store_q)
    loads[1].wait()
    by_head(key_rows, store_k)
    pl.semaphore_wait(barrier, 3 + 15)
    greet_column(plane_in)

    def scatter(first, last, source, target, sent, here, own):
        def column(k, carry):
            column_x = lax.rem(x + k % 4, 4)
            column_y = lax.rem(y + k // 4, 4)
            for j in range(3):
                head, to_span, to_x = place(column_x, column_y, j)
                mine = (to_span == span) & (to_x == x)

                @pl.when(jnp.logical_not(mine))
                def _():
                    pltpu.make_async_remote_copy(
                        source.at[head],
                        target.at[me],
                        sent,
                        here,
                        device_id={"span": to_span, "head": to_x},
                        device_id_type=MESH,
                    ).start()

                @pl.when(mine)
                def _():
                    pltpu.make_async_copy(source.at[head], target.at[me], own).start()

            return carry

        lax.fori_loop(first, last, column, 0)

    scatter(0, 1, send_qk, got_qk, qk_sent, qk_here.at[y], own_qk)
    pl.semaphore_wait(plane_in, 3)
    scatter(1, 16, send_qk, got_qk, qk_sent, qk_here.at[y], own_qk)
    loads[2].wait()
    by_head(value_rows, store_v)
    scatter(0, 16, send_v, got_v, v_sent, v_here.at[y], own_v)

    def wait_for(ref, count, semaphore):
        part = ref.at[pl.ds(0, count)]
        pltpu.make_async_copy(part, part, semaphore).wait()

    @pl.when(active)
    def _():
        def q_of(group, r):
            return got_qk[pl.ds((group * GROUP + r) * QUARTERS, QUARTERS), 0].reshape(SPAN, DIM)

        def keys_of(chunk, spans):
            first = chunk * (GROUP * QUARTERS)
            return got_qk[pl.ds(first, spans * QUARTERS), 1].reshape(spans * SPAN, DIM)

        def values_of(chunk, spans):
            first = chunk * (GROUP * QUARTERS)
            return got_v[pl.ds(first, spans * QUARTERS)].reshape(spans * SPAN, DIM)

        def weigh(pair, r, columns, top):
            ws = [jnp.exp2((s - top) * SCALE) for s in columns]
            for k, w in enumerate(ws):
                weights[pair, r, :, k * BLOCK : (k + 1) * BLOCK] = w.astype(jnp.bfloat16)
            peaks[pair, r] = top
            return fold(ws, jnp.add)

        def own_chunk(group):
            for r in range(GROUP):
                columns = blocks_of(raw_scores(q_of(group, r), keys_of(group, r + 1)))
                hidden = jnp.full((BLOCK, BLOCK), HIDDEN, jnp.float32)
                columns[-1] = jnp.concatenate([hidden, columns[-1][BLOCK:]], axis=0)
                top = jnp.max(fold(columns, jnp.maximum), axis=1, keepdims=True)
                sums[group, r] = weigh(pair_at(group, group), r, columns, top)
                tops[group, r] = top

        def earlier_chunk(group, chunk):
            for r in range(GROUP):
                columns = blocks_of(raw_scores(q_of(group, r), keys_of(chunk, GROUP)))
                before = tops[group, r]
                top = jnp.max(fold(columns, jnp.maximum), axis=1, keepdims=True)
                top = jnp.maximum(before, top)
                added = weigh(pair_at(group, chunk), r, columns, top)
                sums[group, r] = sums[group, r] * jnp.exp2((before - top) * SCALE) + added
                tops[group, r] = top

        def row_of(step):
            return lax.rem(y + CHUNKS - step, CHUNKS)

        def soften(step, carry):
            row = row_of(step)

            @pl.when(step == 0)
            def _():
                wait_for(got_qk, 15, qk_here.at[row])
                wait_for(got_qk, 1, own_qk)

            @pl.when(step > 0)
            def _():
                wait_for(got_qk, 16, qk_here.at[row])

            own_chunk(row)

            def with_row(before, carry):
                other = row_of(before)
                earlier_chunk(jnp.maximum(row, other), jnp.minimum(row, other))
                return carry

            lax.fori_loop(0, step, with_row, 0)
            return carry

        lax.fori_loop(0, CHUNKS, soften, 0)

        def share(group, carry):
            for r in range(GROUP):
                gate = gate_table[noise_levels[group * GROUP + r], my_head]
                shares[group, r] = gate / jnp.sum(sums[group, r], axis=1, keepdims=True)
                acc[group, r] = jnp.zeros((SPAN, DIM), jnp.float32)
            return carry

        lax.fori_loop(0, CHUNKS, share, 0)

        def add_term(group, chunk, spans, r):
            pair = pair_at(group, chunk)
            rescale = jnp.exp2((peaks[pair, r] - tops[group, r]) * SCALE)
            acc[group, r] += rescale * jnp.dot(
                weights[pair, r, :, 0 : spans * SPAN],
                values_of(chunk, spans),
                preferred_element_type=jnp.float32,
            )

        def give_back(group):
            for r in range(GROUP):
                i = group * GROUP + r
                result = (acc[group, r] * shares[group, r]).astype(jnp.bfloat16)
                send_o[pl.ds(i * QUARTERS, QUARTERS)] = result.reshape(QUARTERS, ROWS, DIM)
                for quarter in range(QUARTERS):
                    piece = i * QUARTERS + quarter
                    mine = piece == me

                    @pl.when(jnp.logical_not(mine))
                    def _():
                        pltpu.make_async_remote_copy(
                            send_o.at[piece],
                            got_o.at[my_head],
                            o_sent,
                            o_here,
                            device_id={"span": i, "head": quarter},
                            device_id_type=MESH,
                        ).start()

                    @pl.when(mine)
                    def _():
                        pltpu.make_async_copy(send_o.at[piece], got_o.at[my_head], own_o).start()

        def gather(step, carry):
            row = row_of(step)

            @pl.when(step == 0)
            def _():
                wait_for(got_v, 15, v_here.at[row])
                wait_for(got_v, 1, own_v)

            @pl.when(step > 0)
            def _():
                wait_for(got_v, 16, v_here.at[row])

            def into(group, carry):
                @pl.when(group == row)
                def _():
                    for r in range(GROUP):
                        add_term(group, group, r + 1, r)

                @pl.when(group > row)
                def _():
                    for r in range(GROUP):
                        add_term(group, row, GROUP, r)

                @pl.when(step == jnp.where(group <= y, y, CHUNKS - 1))
                def _():
                    give_back(group)

                return carry

            lax.fori_loop(row, CHUNKS, into, 0)
            return carry

        lax.fori_loop(0, CHUNKS, gather, 0)
        wait_for(got_o, HEADS - 1, o_here)
        wait_for(got_o, 1, own_o)
        wait_for(send_qk, HEADS - 1, qk_sent)
        wait_for(send_v, HEADS - 1, v_sent)
        wait_for(send_o, PEERS - 1, o_sent)

    @pl.when(jnp.logical_not(active))
    def _():
        wait_for(got_o, HEADS, o_here)
        wait_for(send_qk, HEADS, qk_sent)
        wait_for(send_v, HEADS, v_sent)


def body(queries, key_rows, value_rows, noise_levels, gate_table):
    smem = pl.BlockSpec(memory_space=pltpu.SMEM)
    hbm = pl.BlockSpec(memory_space=pl.ANY)
    dma = pltpu.SemaphoreType.DMA
    bf16, f32 = jnp.bfloat16, jnp.float32
    by_head = pl.pallas_call(
        kernel,
        out_shape=jax.ShapeDtypeStruct((HEADS, ROWS, DIM), bf16),
        in_specs=[hbm, hbm, hbm, smem, smem],
        out_specs=hbm,
        scratch_shapes=[pltpu.VMEM((ROWS, HEADS, DIM), bf16)] * 3
        + [
            dma((3,)),
            pltpu.VMEM((ROWS * HEADS, DIM), f32),
            pltpu.VMEM((HEADS, 2, ROWS, DIM), bf16),
            pltpu.VMEM((HEADS, ROWS, DIM), bf16),
            pltpu.VMEM((PEERS, 2, ROWS, DIM), bf16),
            pltpu.VMEM((PEERS, ROWS, DIM), bf16),
            pltpu.VMEM((PAIRS, GROUP, SPAN, CHUNK), bf16),
            pltpu.VMEM((PAIRS, GROUP, SPAN, 1), f32),
            pltpu.VMEM((CHUNKS, GROUP, SPAN, 1), f32),
            pltpu.VMEM((CHUNKS, GROUP, SPAN, 1), f32),
            pltpu.VMEM((CHUNKS, GROUP, SPAN, BLOCK), f32),
            pltpu.VMEM((CHUNKS, GROUP, SPAN, DIM), f32),
            pltpu.VMEM((PEERS, ROWS, DIM), bf16),
        ]
        + [dma, dma((CHUNKS,))] * 2 + [dma] * 5 + [pltpu.SemaphoreType.REGULAR],
        compiler_params=pltpu.CompilerParams(
            collective_id=0, has_side_effects=True, vmem_limit_bytes=56 << 20
        ),
    )(queries, key_rows, value_rows, noise_levels, gate_table)
    return jnp.swapaxes(by_head, 0, 1)


def solution(mesh):
    return jax.shard_map(
        body,
        mesh=mesh,
        in_specs=(
            P(("video", "span", "head"), None, None),
            P(("video", "span", "head"), None, None),
            P(("video", "span", "head"), None, None),
            P("video"),
            P(),
        ),
        out_specs=P(("video", "span", "head"), None, None),
        check_vma=False,
    )
```

```python
import functools
import math

import jax
import jax.numpy as jnp
from jax import lax
from jax.experimental import pallas as pl
from jax.experimental.pallas import tpu as pltpu
from jax.sharding import PartitionSpec as P

MESH = pl.DeviceIdType.MESH
HEADS = 48
DIM = 128
ROWS = 64
SPANS = 16
QUARTERS = 4
SPAN = ROWS * QUARTERS
PEERS = SPANS * QUARTERS
GROUP = 4
CHUNK = SPAN * GROUP
CHUNKS = SPANS // GROUP
BLOCK = 128
HIDDEN = -1e30
SCALE = math.log2(math.e) / math.sqrt(DIM)
PAIRS = CHUNKS * (CHUNKS + 1) // 2


def pair_at(group, chunk):
    return group * (group + 1) // 2 + chunk


def raw_scores(q, keys):
    return lax.dot_general(q, keys, (((1,), (1,)), ((), ())), preferred_element_type=jnp.float32)


def blocks_of(value):
    return [value[:, k * BLOCK : (k + 1) * BLOCK] for k in range(value.shape[1] // BLOCK)]


def fold(parts, op):
    parts = list(parts)
    while len(parts) > 1:
        paired = [op(left, right) for left, right in zip(parts[::2], parts[1::2])]
        parts = paired + (parts[-1:] if len(parts) % 2 else [])
    return parts[0]


def kernel(
    queries_hbm, key_rows_hbm, value_rows_hbm, noise_levels, gate_table, got_o,
    queries, key_rows, value_rows, loaded, wide_q, wide_k, wide_v, send_qk, send_v, got_qk, got_v, weights, peaks, tops, shares, sums, acc, send_o,
    qk_sent, qk_here, v_sent, v_here, o_sent, o_here, own_qk, own_v, own_o, plane_in,
):
    core = lax.axis_index("video") % 2
    span = lax.axis_index("span")
    x = lax.axis_index("head")
    y = span // 4
    z = span % 4
    me = span * QUARTERS + x

    def place(column_x, column_y, j):
        z_at = (j * 3) // 2 + jnp.where(j == 1, core, 0)
        return (column_y * 4 + column_x) * 3 + j, column_y * 4 + z_at, column_x

    j_far = jnp.where(z < 2, 2, 0)
    j_near = jnp.where(z == 0, 0, jnp.where(z == 3, 2, 1))

    def by_distance(turn):
        return jnp.where(turn == 0, j_far, jnp.where(turn == 2, j_near, 3 - j_far - j_near))

    active = (z == 0) | (z == 3) | (z == 1 + core)
    j_mine = jnp.where(z == 0, 0, jnp.where(z == 3, 2, 1))
    my_head = (y * 4 + x) * 3 + j_mine

    loads = [
        pltpu.make_async_copy(source, target, loaded.at[n])
        for n, (source, target) in enumerate(
            [(queries_hbm, queries), (key_rows_hbm, key_rows), (value_rows_hbm, value_rows)]
        )
    ]
    for load in loads:
        load.start()

    barrier = pltpu.get_barrier_semaphore()

    def signal(semaphore, to_span, to_x):
        pl.semaphore_signal(
            semaphore,
            inc=1,
            device_id={"span": to_span, "head": to_x},
            device_id_type=MESH,
        )

    def greet_column(semaphore):
        for i in range(1, 4):
            signal(semaphore, y * 4 + lax.rem(z + i, 4), x)

    greet_column(barrier)
    for i in range(1, 16):
        signal(barrier, lax.rem(y + i // 4, 4) * 4 + z, lax.rem(x + i % 4, 4))

    def widen(ref, wide):
        wide[...] = ref[...].reshape(ROWS * HEADS, DIM).astype(jnp.float32)

    def head_of(wide, head):
        return wide[pl.ds(head, ROWS, stride=HEADS), :].astype(jnp.bfloat16)

    def lay_out_qk(head):
        send_qk[head, 0] = head_of(wide_q, head)
        send_qk[head, 1] = head_of(wide_k, head)

    def lay_out_v(head):
        send_v[head] = head_of(wide_v, head)

    loads[0].wait()
    widen(queries, wide_q)
    loads[1].wait()
    widen(key_rows, wide_k)
    pl.semaphore_wait(barrier, 3 + 15)
    greet_column(plane_in)

    def send_one(k, turn, lay_out, source, target, sent, here, own):
        column_x = lax.rem(x + k % 4, 4)
        column_y = lax.rem(y + k // 4, 4)
        head, to_span, to_x = place(column_x, column_y, by_distance(turn))
        lay_out(head)
        mine = (to_span == span) & (to_x == x)

        @pl.when(jnp.logical_not(mine))
        def _():
            pltpu.make_async_remote_copy(
                source.at[head],
                target.at[me],
                sent,
                here,
                device_id={"span": to_span, "head": to_x},
                device_id_type=MESH,
            ).start()

        @pl.when(mine)
        def _():
            pltpu.make_async_copy(source.at[head], target.at[me], own).start()

    def scatter_column(*way):
        def one(turn, carry):
            send_one(0, turn, *way)
            return carry

        lax.fori_loop(0, 3, one, 0)

    def scatter_rest(*way):
        def one(n, carry):
            k = (n // 12) * 4 + n % 4
            turn = 2 - (n % 12) // 4

            @pl.when(k > 0)
            def _():
                send_one(k, turn, *way)

            return carry

        lax.fori_loop(0, HEADS, one, 0)

    way_qk = (lay_out_qk, send_qk, got_qk, qk_sent, qk_here.at[y], own_qk)
    way_v = (lay_out_v, send_v, got_v, v_sent, v_here.at[y], own_v)

    def wait_for(ref, count, semaphore):
        part = ref.at[pl.ds(0, count)]
        pltpu.make_async_copy(part, part, semaphore).wait()

    scatter_column(*way_qk)
    loads[2].wait()
    widen(value_rows, wide_v)
    scatter_column(*way_v)
    pl.semaphore_wait(plane_in, 3)
    scatter_rest(*way_qk)
    scatter_rest(*way_v)

    @pl.when(active)
    def _():
        def q_of(group, r):
            return got_qk[pl.ds((group * GROUP + r) * QUARTERS, QUARTERS), 0].reshape(SPAN, DIM)

        def keys_of(chunk, spans):
            first = chunk * (GROUP * QUARTERS)
            return got_qk[pl.ds(first, spans * QUARTERS), 1].reshape(spans * SPAN, DIM)

        def values_of(chunk, spans):
            first = chunk * (GROUP * QUARTERS)
            return got_v[pl.ds(first, spans * QUARTERS)].reshape(spans * SPAN, DIM)

        def weigh(pair, r, columns, top):
            ws = [jnp.exp2((s - top) * SCALE) for s in columns]
            for k, w in enumerate(ws):
                weights[pair, r, :, k * BLOCK : (k + 1) * BLOCK] = w.astype(jnp.bfloat16)
            peaks[pair, r] = top
            return fold(ws, jnp.add)

        def own_chunk(group):
            for r in range(GROUP):
                columns = blocks_of(raw_scores(q_of(group, r), keys_of(group, r + 1)))
                hidden = jnp.full((BLOCK, BLOCK), HIDDEN, jnp.float32)
                columns[-1] = jnp.concatenate([hidden, columns[-1][BLOCK:]], axis=0)
                top = jnp.max(fold(columns, jnp.maximum), axis=1, keepdims=True)
                sums[group, r] = weigh(pair_at(group, group), r, columns, top)
                tops[group, r] = top

        def earlier_chunk(group, chunk):
            for r in range(GROUP):
                columns = blocks_of(raw_scores(q_of(group, r), keys_of(chunk, GROUP)))
                before = tops[group, r]
                top = jnp.max(fold(columns, jnp.maximum), axis=1, keepdims=True)
                top = jnp.maximum(before, top)
                added = weigh(pair_at(group, chunk), r, columns, top)
                sums[group, r] = sums[group, r] * jnp.exp2((before - top) * SCALE) + added
                tops[group, r] = top

        def row_of(step):
            return lax.rem(y + CHUNKS - step, CHUNKS)

        def soften(step, carry):
            row = row_of(step)

            @pl.when(step == 0)
            def _():
                wait_for(got_qk, 15, qk_here.at[row])
                wait_for(got_qk, 1, own_qk)

            @pl.when(step > 0)
            def _():
                wait_for(got_qk, 16, qk_here.at[row])

            own_chunk(row)

            def with_row(before, carry):
                other = row_of(before)
                earlier_chunk(jnp.maximum(row, other), jnp.minimum(row, other))
                return carry

            lax.fori_loop(0, step, with_row, 0)
            return carry

        lax.fori_loop(0, CHUNKS, soften, 0)

        def share(group, carry):
            for r in range(GROUP):
                gate = gate_table[noise_levels[group * GROUP + r], my_head]
                shares[group, r] = gate / jnp.sum(sums[group, r], axis=1, keepdims=True)
                acc[group, r] = jnp.zeros((SPAN, DIM), jnp.float32)
            return carry

        lax.fori_loop(0, CHUNKS, share, 0)

        def add_term(group, chunk, spans, r):
            pair = pair_at(group, chunk)
            rescale = jnp.exp2((peaks[pair, r] - tops[group, r]) * SCALE)
            acc[group, r] += rescale * jnp.dot(
                weights[pair, r, :, 0 : spans * SPAN],
                values_of(chunk, spans),
                preferred_element_type=jnp.float32,
            )

        def give_back(group):
            for r in range(GROUP):
                i = group * GROUP + r
                result = (acc[group, r] * shares[group, r]).astype(jnp.bfloat16)
                send_o[pl.ds(i * QUARTERS, QUARTERS)] = result.reshape(QUARTERS, ROWS, DIM)
                for quarter in range(QUARTERS):
                    piece = i * QUARTERS + quarter
                    mine = piece == me

                    @pl.when(jnp.logical_not(mine))
                    def _():
                        pltpu.make_async_remote_copy(
                            send_o.at[piece],
                            got_o.at[my_head],
                            o_sent,
                            o_here,
                            device_id={"span": i, "head": quarter},
                            device_id_type=MESH,
                        ).start()

                    @pl.when(mine)
                    def _():
                        pltpu.make_async_copy(send_o.at[piece], got_o.at[my_head], own_o).start()

        def gather(step, carry):
            row = row_of(step)

            @pl.when(step == 0)
            def _():
                wait_for(got_v, 15, v_here.at[row])
                wait_for(got_v, 1, own_v)

            @pl.when(step > 0)
            def _():
                wait_for(got_v, 16, v_here.at[row])

            def into(group, carry):
                @pl.when(group == row)
                def _():
                    for r in range(GROUP):
                        add_term(group, group, r + 1, r)

                @pl.when(group > row)
                def _():
                    for r in range(GROUP):
                        add_term(group, row, GROUP, r)

                @pl.when(step == jnp.where(group <= y, y, CHUNKS - 1))
                def _():
                    give_back(group)

                return carry

            lax.fori_loop(row, CHUNKS, into, 0)
            return carry

        lax.fori_loop(0, CHUNKS, gather, 0)
        wait_for(got_o, HEADS - 1, o_here)
        wait_for(got_o, 1, own_o)
        wait_for(send_qk, HEADS - 1, qk_sent)
        wait_for(send_v, HEADS - 1, v_sent)
        wait_for(send_o, PEERS - 1, o_sent)

    @pl.when(jnp.logical_not(active))
    def _():
        wait_for(got_o, HEADS, o_here)
        wait_for(send_qk, HEADS, qk_sent)
        wait_for(send_v, HEADS, v_sent)


def body(queries, key_rows, value_rows, noise_levels, gate_table):
    smem = pl.BlockSpec(memory_space=pltpu.SMEM)
    hbm = pl.BlockSpec(memory_space=pl.ANY)
    dma = pltpu.SemaphoreType.DMA
    bf16, f32 = jnp.bfloat16, jnp.float32
    by_head = pl.pallas_call(
        kernel,
        out_shape=jax.ShapeDtypeStruct((HEADS, ROWS, DIM), bf16),
        in_specs=[hbm, hbm, hbm, smem, smem],
        out_specs=hbm,
        scratch_shapes=[pltpu.VMEM((ROWS, HEADS, DIM), bf16)] * 3
        + [
            dma((3,)),
            pltpu.VMEM((ROWS * HEADS, DIM), f32),
            pltpu.VMEM((ROWS * HEADS, DIM), f32),
            pltpu.VMEM((ROWS * HEADS, DIM), f32),
            pltpu.VMEM((HEADS, 2, ROWS, DIM), bf16),
            pltpu.VMEM((HEADS, ROWS, DIM), bf16),
            pltpu.VMEM((PEERS, 2, ROWS, DIM), bf16),
            pltpu.VMEM((PEERS, ROWS, DIM), bf16),
            pltpu.VMEM((PAIRS, GROUP, SPAN, CHUNK), bf16),
            pltpu.VMEM((PAIRS, GROUP, SPAN, 1), f32),
            pltpu.VMEM((CHUNKS, GROUP, SPAN, 1), f32),
            pltpu.VMEM((CHUNKS, GROUP, SPAN, 1), f32),
            pltpu.VMEM((CHUNKS, GROUP, SPAN, BLOCK), f32),
            pltpu.VMEM((CHUNKS, GROUP, SPAN, DIM), f32),
            pltpu.VMEM((PEERS, ROWS, DIM), bf16),
        ]
        + [dma, dma((CHUNKS,))] * 2 + [dma] * 5 + [pltpu.SemaphoreType.REGULAR],
        compiler_params=pltpu.CompilerParams(
            collective_id=0, has_side_effects=True, vmem_limit_bytes=56 << 20
        ),
    )(queries, key_rows, value_rows, noise_levels, gate_table)
    return jnp.swapaxes(by_head, 0, 1)


def solution(mesh):
    return jax.shard_map(
        body,
        mesh=mesh,
        in_specs=(
            P(("video", "span", "head"), None, None),
            P(("video", "span", "head"), None, None),
            P(("video", "span", "head"), None, None),
            P("video"),
            P(),
        ),
        out_specs=P(("video", "span", "head"), None, None),
        check_vma=False,
    )
```

```python
import functools
import math

import jax
import jax.numpy as jnp
from jax import lax
from jax.experimental import pallas as pl
from jax.experimental.pallas import tpu as pltpu
from jax.sharding import PartitionSpec as P

MESH = pl.DeviceIdType.MESH
HEADS = 48
DIM = 128
ROWS = 64
SPANS = 16
QUARTERS = 4
SPAN = ROWS * QUARTERS
PEERS = SPANS * QUARTERS
GROUP = 4
CHUNK = SPAN * GROUP
CHUNKS = SPANS // GROUP
BLOCK = 128
HIDDEN = -1e30
SCALE = math.log2(math.e) / math.sqrt(DIM)
PAIRS = CHUNKS * (CHUNKS + 1) // 2


def pair_at(group, chunk):
    return group * (group + 1) // 2 + chunk


def raw_scores(q, keys):
    return lax.dot_general(q, keys, (((1,), (1,)), ((), ())), preferred_element_type=jnp.float32)


def blocks_of(value):
    return [value[:, k * BLOCK : (k + 1) * BLOCK] for k in range(value.shape[1] // BLOCK)]


def fold(parts, op):
    parts = list(parts)
    while len(parts) > 1:
        paired = [op(left, right) for left, right in zip(parts[::2], parts[1::2])]
        parts = paired + (parts[-1:] if len(parts) % 2 else [])
    return parts[0]


def kernel(
    queries_hbm, key_rows_hbm, value_rows_hbm, noise_levels_hbm, gate_table_hbm, got_o,
    queries, key_rows, value_rows, noise_levels, gate_table, loaded, wide_q, wide_k, wide_v, send_qk, send_v, got_qk, got_v, weights, peaks, tops, shares, sums, acc, send_o,
    qk_sent, qk_here, v_sent, v_here, o_sent, o_here, own_qk, own_v, own_o, plane_in,
):
    core = lax.axis_index("video") % 2
    span = lax.axis_index("span")
    x = lax.axis_index("head")
    y = span // 4
    z = span % 4
    me = span * QUARTERS + x

    def place(column_x, column_y, j):
        z_at = (j * 3) // 2 + jnp.where(j == 1, core, 0)
        return (column_y * 4 + column_x) * 3 + j, column_y * 4 + z_at, column_x

    j_far = jnp.where(z < 2, 2, 0)
    j_near = jnp.where(z == 0, 0, jnp.where(z == 3, 2, 1))

    def by_distance(turn):
        return jnp.where(turn == 0, j_far, jnp.where(turn == 2, j_near, 3 - j_far - j_near))

    active = (z == 0) | (z == 3) | (z == 1 + core)
    j_mine = jnp.where(z == 0, 0, jnp.where(z == 3, 2, 1))
    my_head = (y * 4 + x) * 3 + j_mine

    loads = [
        pltpu.make_async_copy(source, target, loaded.at[n])
        for n, (source, target) in enumerate(
            [
                (queries_hbm, queries),
                (key_rows_hbm, key_rows),
                (value_rows_hbm, value_rows),
                (noise_levels_hbm, noise_levels),
                (gate_table_hbm, gate_table),
            ]
        )
    ]
    for load in loads:
        load.start()

    barrier = pltpu.get_barrier_semaphore()

    def signal(semaphore, to_span, to_x):
        pl.semaphore_signal(
            semaphore,
            inc=1,
            device_id={"span": to_span, "head": to_x},
            device_id_type=MESH,
        )

    def greet_column(semaphore):
        for i in range(1, 4):
            signal(semaphore, y * 4 + lax.rem(z + i, 4), x)

    greet_column(barrier)
    for i in range(1, 16):
        signal(barrier, lax.rem(y + i // 4, 4) * 4 + z, lax.rem(x + i % 4, 4))

    def widen(ref, wide):
        wide[...] = ref[...].reshape(ROWS * HEADS, DIM).astype(jnp.float32)

    def head_of(wide, head):
        return wide[pl.ds(head, ROWS, stride=HEADS), :].astype(jnp.bfloat16)

    def lay_out_qk(head):
        send_qk[head, 0] = head_of(wide_q, head)
        send_qk[head, 1] = head_of(wide_k, head)

    def lay_out_v(head):
        send_v[head] = head_of(wide_v, head)

    loads[0].wait()
    widen(queries, wide_q)
    loads[1].wait()
    widen(key_rows, wide_k)
    pl.semaphore_wait(barrier, 3 + 15)
    greet_column(plane_in)

    def send_one(k, turn, lay_out, source, target, sent, here, own):
        column_x = lax.rem(x + k % 4, 4)
        column_y = lax.rem(y + k // 4, 4)
        head, to_span, to_x = place(column_x, column_y, by_distance(turn))
        lay_out(head)
        mine = (to_span == span) & (to_x == x)

        @pl.when(jnp.logical_not(mine))
        def _():
            pltpu.make_async_remote_copy(
                source.at[head],
                target.at[me],
                sent,
                here,
                device_id={"span": to_span, "head": to_x},
                device_id_type=MESH,
            ).start()

        @pl.when(mine)
        def _():
            pltpu.make_async_copy(source.at[head], target.at[me], own).start()

    def scatter_column(*way):
        def one(turn, carry):
            send_one(0, turn, *way)
            return carry

        lax.fori_loop(0, 3, one, 0)

    def scatter_rest(order, *way):
        def one(n, carry):
            k, turn = order(n)

            @pl.when(k > 0)
            def _():
                send_one(k, turn, *way)

            return carry

        lax.fori_loop(0, HEADS, one, 0)

    way_qk = (lay_out_qk, send_qk, got_qk, qk_sent, qk_here.at[y], own_qk)
    way_v = (lay_out_v, send_v, got_v, v_sent, v_here.at[y], own_v)

    def wait_for(ref, count, semaphore):
        part = ref.at[pl.ds(0, count)]
        pltpu.make_async_copy(part, part, semaphore).wait()

    scatter_column(*way_qk)
    for load in loads[2:]:
        load.wait()
    widen(value_rows, wide_v)
    scatter_column(*way_v)
    pl.semaphore_wait(plane_in, 3)
    def rows_near(n):
        return (n // 12) * 4 + n % 4, 2 - (n % 12) // 4

    def rows_v(n):
        return n % 16, 2 - n // 16

    scatter_rest(rows_near, *way_qk)
    scatter_rest(rows_v, *way_v)

    @pl.when(active)
    def _():
        def q_of(group, r):
            return got_qk[pl.ds((group * GROUP + r) * QUARTERS, QUARTERS), 0].reshape(SPAN, DIM)

        def keys_of(chunk, spans):
            first = chunk * (GROUP * QUARTERS)
            return got_qk[pl.ds(first, spans * QUARTERS), 1].reshape(spans * SPAN, DIM)

        def values_of(chunk, spans):
            first = chunk * (GROUP * QUARTERS)
            return got_v[pl.ds(first, spans * QUARTERS)].reshape(spans * SPAN, DIM)

        def weigh(pair, r, columns, top):
            ws = [jnp.exp2((s - top) * SCALE) for s in columns]
            for k, w in enumerate(ws):
                weights[pair, r, :, k * BLOCK : (k + 1) * BLOCK] = w.astype(jnp.bfloat16)
            peaks[pair, r] = top
            return fold(ws, jnp.add)

        def own_chunk(group):
            for r in range(GROUP):
                columns = blocks_of(raw_scores(q_of(group, r), keys_of(group, r + 1)))
                hidden = jnp.full((BLOCK, BLOCK), HIDDEN, jnp.float32)
                columns[-1] = jnp.concatenate([hidden, columns[-1][BLOCK:]], axis=0)
                top = jnp.max(fold(columns, jnp.maximum), axis=1, keepdims=True)
                sums[group, r] = weigh(pair_at(group, group), r, columns, top)
                tops[group, r] = top

        def earlier_chunk(group, chunk):
            for r in range(GROUP):
                columns = blocks_of(raw_scores(q_of(group, r), keys_of(chunk, GROUP)))
                before = tops[group, r]
                top = jnp.max(fold(columns, jnp.maximum), axis=1, keepdims=True)
                top = jnp.maximum(before, top)
                added = weigh(pair_at(group, chunk), r, columns, top)
                sums[group, r] = sums[group, r] * jnp.exp2((before - top) * SCALE) + added
                tops[group, r] = top

        def row_of(step):
            return lax.rem(y + CHUNKS - step, CHUNKS)

        def soften(step, carry):
            row = row_of(step)

            @pl.when(step == 0)
            def _():
                wait_for(got_qk, 15, qk_here.at[row])
                wait_for(got_qk, 1, own_qk)

            @pl.when(step > 0)
            def _():
                wait_for(got_qk, 16, qk_here.at[row])

            own_chunk(row)

            def with_row(before, carry):
                other = row_of(before)
                earlier_chunk(jnp.maximum(row, other), jnp.minimum(row, other))
                return carry

            lax.fori_loop(0, step, with_row, 0)
            return carry

        lax.fori_loop(0, CHUNKS, soften, 0)

        def share(group, carry):
            for r in range(GROUP):
                gate = gate_table[noise_levels[group * GROUP + r], my_head]
                shares[group, r] = gate / jnp.sum(sums[group, r], axis=1, keepdims=True)
                acc[group, r] = jnp.zeros((SPAN, DIM), jnp.float32)
            return carry

        lax.fori_loop(0, CHUNKS, share, 0)

        def add_term(group, chunk, spans, r):
            pair = pair_at(group, chunk)
            rescale = jnp.exp2((peaks[pair, r] - tops[group, r]) * SCALE)
            acc[group, r] += rescale * jnp.dot(
                weights[pair, r, :, 0 : spans * SPAN],
                values_of(chunk, spans),
                preferred_element_type=jnp.float32,
            )

        def give_back(group):
            for r in range(GROUP):
                i = group * GROUP + r
                result = (acc[group, r] * shares[group, r]).astype(jnp.bfloat16)
                send_o[pl.ds(i * QUARTERS, QUARTERS)] = result.reshape(QUARTERS, ROWS, DIM)
                for quarter in range(QUARTERS):
                    piece = i * QUARTERS + quarter
                    mine = piece == me

                    @pl.when(jnp.logical_not(mine))
                    def _():
                        pltpu.make_async_remote_copy(
                            send_o.at[piece],
                            got_o.at[my_head],
                            o_sent,
                            o_here,
                            device_id={"span": i, "head": quarter},
                            device_id_type=MESH,
                        ).start()

                    @pl.when(mine)
                    def _():
                        pltpu.make_async_copy(send_o.at[piece], got_o.at[my_head], own_o).start()

        def gather(step, carry):
            row = row_of(step)

            @pl.when(step == 0)
            def _():
                wait_for(got_v, 15, v_here.at[row])
                wait_for(got_v, 1, own_v)

            @pl.when(step > 0)
            def _():
                wait_for(got_v, 16, v_here.at[row])

            def into(group, carry):
                @pl.when(group == row)
                def _():
                    for r in range(GROUP):
                        add_term(group, group, r + 1, r)

                @pl.when(group > row)
                def _():
                    for r in range(GROUP):
                        add_term(group, row, GROUP, r)

                @pl.when(step == jnp.where(group <= y, y, CHUNKS - 1))
                def _():
                    give_back(group)

                return carry

            lax.fori_loop(row, CHUNKS, into, 0)
            return carry

        lax.fori_loop(0, CHUNKS, gather, 0)
        wait_for(got_o, HEADS - 1, o_here)
        wait_for(got_o, 1, own_o)
        wait_for(send_qk, HEADS - 1, qk_sent)
        wait_for(send_v, HEADS - 1, v_sent)
        wait_for(send_o, PEERS - 1, o_sent)

    @pl.when(jnp.logical_not(active))
    def _():
        wait_for(got_o, HEADS, o_here)
        wait_for(send_qk, HEADS, qk_sent)
        wait_for(send_v, HEADS, v_sent)


def body(*operands):
    hbm = pl.BlockSpec(memory_space=pltpu.HBM)
    anywhere = pl.BlockSpec(memory_space=pl.ANY)
    dma = pltpu.SemaphoreType.DMA
    bf16, f32 = jnp.bfloat16, jnp.float32
    by_head = pl.pallas_call(
        kernel,
        out_shape=jax.ShapeDtypeStruct((HEADS, ROWS, DIM), bf16),
        in_specs=[hbm] * 5,
        out_specs=anywhere,
        scratch_shapes=[pltpu.VMEM((ROWS, HEADS, DIM), bf16)] * 3
        + [
            pltpu.SMEM((SPANS,), jnp.int32),
            pltpu.SMEM((8, HEADS), f32),
            dma((5,)),
            pltpu.VMEM((ROWS * HEADS, DIM), f32),
            pltpu.VMEM((ROWS * HEADS, DIM), f32),
            pltpu.VMEM((ROWS * HEADS, DIM), f32),
            pltpu.VMEM((HEADS, 2, ROWS, DIM), bf16),
            pltpu.VMEM((HEADS, ROWS, DIM), bf16),
            pltpu.VMEM((PEERS, 2, ROWS, DIM), bf16),
            pltpu.VMEM((PEERS, ROWS, DIM), bf16),
            pltpu.VMEM((PAIRS, GROUP, SPAN, CHUNK), bf16),
            pltpu.VMEM((PAIRS, GROUP, SPAN, 1), f32),
            pltpu.VMEM((CHUNKS, GROUP, SPAN, 1), f32),
            pltpu.VMEM((CHUNKS, GROUP, SPAN, 1), f32),
            pltpu.VMEM((CHUNKS, GROUP, SPAN, BLOCK), f32),
            pltpu.VMEM((CHUNKS, GROUP, SPAN, DIM), f32),
            pltpu.VMEM((PEERS, ROWS, DIM), bf16),
        ]
        + [dma, dma((CHUNKS,))] * 2 + [dma] * 5 + [pltpu.SemaphoreType.REGULAR],
        compiler_params=pltpu.CompilerParams(
            collective_id=0, has_side_effects=True, vmem_limit_bytes=53 << 20
        ),
    )(*[pltpu.with_memory_space_constraint(operand, pltpu.HBM) for operand in operands])
    return jnp.swapaxes(by_head, 0, 1)


def solution(mesh):
    return jax.shard_map(
        body,
        mesh=mesh,
        in_specs=(
            P(("video", "span", "head"), None, None),
            P(("video", "span", "head"), None, None),
            P(("video", "span", "head"), None, None),
            P("video"),
            P(),
        ),
        out_specs=P(("video", "span", "head"), None, None),
        check_vma=False,
    )
```

```python
import functools
import math

import jax
import jax.numpy as jnp
from jax import lax
from jax.experimental import pallas as pl
from jax.experimental.pallas import tpu as pltpu
from jax.sharding import PartitionSpec as P

MESH = pl.DeviceIdType.MESH
HEADS = 48
DIM = 128
ROWS = 64
SPANS = 16
QUARTERS = 4
SPAN = ROWS * QUARTERS
PEERS = SPANS * QUARTERS
GROUP = 4
CHUNK = SPAN * GROUP
CHUNKS = SPANS // GROUP
BLOCK = 128
HIDDEN = -1e30
SCALE = math.log2(math.e) / math.sqrt(DIM)
PAIRS = CHUNKS * (CHUNKS + 1) // 2


def pair_at(group, chunk):
    return group * (group + 1) // 2 + chunk


def raw_scores(q, keys):
    return lax.dot_general(q, keys, (((1,), (1,)), ((), ())), preferred_element_type=jnp.float32)


def blocks_of(value):
    return [value[:, k * BLOCK : (k + 1) * BLOCK] for k in range(value.shape[1] // BLOCK)]


def fold(parts, op):
    parts = list(parts)
    while len(parts) > 1:
        paired = [op(left, right) for left, right in zip(parts[::2], parts[1::2])]
        parts = paired + (parts[-1:] if len(parts) % 2 else [])
    return parts[0]


def kernel(
    queries_hbm, key_rows_hbm, value_rows_hbm, noise_levels_hbm, gate_table_hbm, got_o,
    queries, key_rows, value_rows, noise_levels, gate_table, loaded, wide_q, wide_k, wide_v, send_qk, send_v, got_qk, got_v, weights, peaks, tops, shares, sums, acc, send_o,
    qk_sent, qk_here, v_sent, v_here, o_sent, o_here, own_qk, own_v, own_o, plane_in,
):
    core = lax.axis_index("video") % 2
    span = lax.axis_index("span")
    x = lax.axis_index("head")
    y = span // 4
    z = span % 4
    me = span * QUARTERS + x

    def place(column_x, column_y, j):
        z_at = (j * 3) // 2 + jnp.where(j == 1, core, 0)
        return (column_y * 4 + column_x) * 3 + j, column_y * 4 + z_at, column_x

    j_far = jnp.where(z < 2, 2, 0)
    j_near = jnp.where(z == 0, 0, jnp.where(z == 3, 2, 1))

    def by_distance(turn):
        return jnp.where(turn == 0, j_far, jnp.where(turn == 2, j_near, 3 - j_far - j_near))

    active = (z == 0) | (z == 3) | (z == 1 + core)
    j_mine = jnp.where(z == 0, 0, jnp.where(z == 3, 2, 1))
    my_head = (y * 4 + x) * 3 + j_mine

    loads = [
        pltpu.make_async_copy(source, target, loaded.at[n])
        for n, (source, target) in enumerate(
            [
                (queries_hbm, queries),
                (key_rows_hbm, key_rows),
                (value_rows_hbm, value_rows),
                (noise_levels_hbm, noise_levels),
                (gate_table_hbm, gate_table),
            ]
        )
    ]
    for load in loads:
        load.start()

    barrier = pltpu.get_barrier_semaphore()

    def signal(semaphore, to_span, to_x):
        pl.semaphore_signal(
            semaphore,
            inc=1,
            device_id={"span": to_span, "head": to_x},
            device_id_type=MESH,
        )

    def greet_column(semaphore):
        for i in range(1, 4):
            signal(semaphore, y * 4 + lax.rem(z + i, 4), x)

    greet_column(barrier)
    for i in range(1, 16):
        signal(barrier, lax.rem(y + i // 4, 4) * 4 + z, lax.rem(x + i % 4, 4))

    def widen(ref, wide):
        wide[...] = ref[...].reshape(ROWS * HEADS, DIM).astype(jnp.float32)

    def head_of(wide, head):
        return wide[pl.ds(head, ROWS, stride=HEADS), :].astype(jnp.bfloat16)

    def lay_out_qk(head):
        send_qk[head, 0] = head_of(wide_q, head)
        send_qk[head, 1] = head_of(wide_k, head)

    def lay_out_v(head):
        send_v[head] = head_of(wide_v, head)

    loads[0].wait()
    widen(queries, wide_q)
    loads[1].wait()
    widen(key_rows, wide_k)
    pl.semaphore_wait(barrier, 3 + 15)
    greet_column(plane_in)

    def send_one(k, turn, stride_y, lay_out, source, target, sent, here, own):
        column_x = lax.rem(x + k % 4, 4)
        column_y = lax.rem(y + stride_y * (k // 4), 4)
        head, to_span, to_x = place(column_x, column_y, by_distance(turn))
        lay_out(head)
        mine = (to_span == span) & (to_x == x)

        @pl.when(jnp.logical_not(mine))
        def _():
            pltpu.make_async_remote_copy(
                source.at[head],
                target.at[me],
                sent,
                here,
                device_id={"span": to_span, "head": to_x},
                device_id_type=MESH,
            ).start()

        @pl.when(mine)
        def _():
            pltpu.make_async_copy(source.at[head], target.at[me], own).start()

    def scatter_column(*way):
        def one(turn, carry):
            send_one(0, turn, *way)
            return carry

        lax.fori_loop(0, 3, one, 0)

    def scatter_rest(order, *way):
        def one(n, carry):
            k, turn = order(n)

            @pl.when(k > 0)
            def _():
                send_one(k, turn, *way)

            return carry

        lax.fori_loop(0, HEADS, one, 0)

    way_qk = (3, lay_out_qk, send_qk, got_qk, qk_sent, qk_here.at[y], own_qk)
    way_v = (1, lay_out_v, send_v, got_v, v_sent, v_here.at[y], own_v)

    def wait_for(ref, count, semaphore):
        part = ref.at[pl.ds(0, count)]
        pltpu.make_async_copy(part, part, semaphore).wait()

    scatter_column(*way_qk)
    for load in loads[2:]:
        load.wait()
    widen(value_rows, wide_v)
    scatter_column(*way_v)
    pl.semaphore_wait(plane_in, 3)
    def rows_near(n):
        return (n // 12) * 4 + n % 4, 2 - (n % 12) // 4

    def rows_v(n):
        return n % 16, 2 - n // 16

    scatter_rest(rows_near, *way_qk)
    scatter_rest(rows_v, *way_v)

    @pl.when(active)
    def _():
        def q_of(group, r):
            return got_qk[pl.ds((group * GROUP + r) * QUARTERS, QUARTERS), 0].reshape(SPAN, DIM)

        def keys_of(chunk, spans):
            first = chunk * (GROUP * QUARTERS)
            return got_qk[pl.ds(first, spans * QUARTERS), 1].reshape(spans * SPAN, DIM)

        def values_of(chunk, spans):
            first = chunk * (GROUP * QUARTERS)
            return got_v[pl.ds(first, spans * QUARTERS)].reshape(spans * SPAN, DIM)

        def weigh(pair, r, columns, top):
            ws = [jnp.exp2((s - top) * SCALE) for s in columns]
            for k, w in enumerate(ws):
                weights[pair, r, :, k * BLOCK : (k + 1) * BLOCK] = w.astype(jnp.bfloat16)
            peaks[pair, r] = top
            return fold(ws, jnp.add)

        def own_chunk(group):
            for r in range(GROUP):
                columns = blocks_of(raw_scores(q_of(group, r), keys_of(group, r + 1)))
                hidden = jnp.full((BLOCK, BLOCK), HIDDEN, jnp.float32)
                columns[-1] = jnp.concatenate([hidden, columns[-1][BLOCK:]], axis=0)
                top = jnp.max(fold(columns, jnp.maximum), axis=1, keepdims=True)
                sums[group, r] = weigh(pair_at(group, group), r, columns, top)
                tops[group, r] = top

        def earlier_chunk(group, chunk):
            for r in range(GROUP):
                columns = blocks_of(raw_scores(q_of(group, r), keys_of(chunk, GROUP)))
                before = tops[group, r]
                top = jnp.max(fold(columns, jnp.maximum), axis=1, keepdims=True)
                top = jnp.maximum(before, top)
                added = weigh(pair_at(group, chunk), r, columns, top)
                sums[group, r] = sums[group, r] * jnp.exp2((before - top) * SCALE) + added
                tops[group, r] = top

        def row_of(step):
            return lax.rem(y + step, CHUNKS)

        def soften(step, carry):
            row = row_of(step)

            @pl.when(step == 0)
            def _():
                wait_for(got_qk, 15, qk_here.at[row])
                wait_for(got_qk, 1, own_qk)

            @pl.when(step > 0)
            def _():
                wait_for(got_qk, 16, qk_here.at[row])

            own_chunk(row)

            def with_row(before, carry):
                other = row_of(before)
                earlier_chunk(jnp.maximum(row, other), jnp.minimum(row, other))
                return carry

            lax.fori_loop(0, step, with_row, 0)
            return carry

        lax.fori_loop(0, CHUNKS, soften, 0)

        def share(group, carry):
            for r in range(GROUP):
                gate = gate_table[noise_levels[group * GROUP + r], my_head]
                shares[group, r] = gate / jnp.sum(sums[group, r], axis=1, keepdims=True)
                acc[group, r] = jnp.zeros((SPAN, DIM), jnp.float32)
            return carry

        lax.fori_loop(0, CHUNKS, share, 0)

        def add_term(group, chunk, spans, r):
            pair = pair_at(group, chunk)
            rescale = jnp.exp2((peaks[pair, r] - tops[group, r]) * SCALE)
            acc[group, r] += rescale * jnp.dot(
                weights[pair, r, :, 0 : spans * SPAN],
                values_of(chunk, spans),
                preferred_element_type=jnp.float32,
            )

        def give_back(group):
            for r in range(GROUP):
                i = group * GROUP + r
                result = (acc[group, r] * shares[group, r]).astype(jnp.bfloat16)
                send_o[pl.ds(i * QUARTERS, QUARTERS)] = result.reshape(QUARTERS, ROWS, DIM)
                for quarter in range(QUARTERS):
                    piece = i * QUARTERS + quarter
                    mine = piece == me

                    @pl.when(jnp.logical_not(mine))
                    def _():
                        pltpu.make_async_remote_copy(
                            send_o.at[piece],
                            got_o.at[my_head],
                            o_sent,
                            o_here,
                            device_id={"span": i, "head": quarter},
                            device_id_type=MESH,
                        ).start()

                    @pl.when(mine)
                    def _():
                        pltpu.make_async_copy(send_o.at[piece], got_o.at[my_head], own_o).start()

        def gather(step, carry):
            row = lax.rem(y + CHUNKS - step, CHUNKS)

            @pl.when(step == 0)
            def _():
                wait_for(got_v, 15, v_here.at[row])
                wait_for(got_v, 1, own_v)

            @pl.when(step > 0)
            def _():
                wait_for(got_v, 16, v_here.at[row])

            def into(group, carry):
                @pl.when(group == row)
                def _():
                    for r in range(GROUP):
                        add_term(group, group, r + 1, r)

                @pl.when(group > row)
                def _():
                    for r in range(GROUP):
                        add_term(group, row, GROUP, r)

                @pl.when(step == jnp.where(group <= y, y, CHUNKS - 1))
                def _():
                    give_back(group)

                return carry

            lax.fori_loop(row, CHUNKS, into, 0)
            return carry

        lax.fori_loop(0, CHUNKS, gather, 0)
        wait_for(got_o, HEADS - 1, o_here)
        wait_for(got_o, 1, own_o)
        wait_for(send_qk, HEADS - 1, qk_sent)
        wait_for(send_v, HEADS - 1, v_sent)
        wait_for(send_o, PEERS - 1, o_sent)

    @pl.when(jnp.logical_not(active))
    def _():
        wait_for(got_o, HEADS, o_here)
        wait_for(send_qk, HEADS, qk_sent)
        wait_for(send_v, HEADS, v_sent)


def body(*operands):
    hbm = pl.BlockSpec(memory_space=pltpu.HBM)
    anywhere = pl.BlockSpec(memory_space=pl.ANY)
    dma = pltpu.SemaphoreType.DMA
    bf16, f32 = jnp.bfloat16, jnp.float32
    by_head = pl.pallas_call(
        kernel,
        out_shape=jax.ShapeDtypeStruct((HEADS, ROWS, DIM), bf16),
        in_specs=[hbm] * 5,
        out_specs=anywhere,
        scratch_shapes=[pltpu.VMEM((ROWS, HEADS, DIM), bf16)] * 3
        + [
            pltpu.SMEM((SPANS,), jnp.int32),
            pltpu.SMEM((8, HEADS), f32),
            dma((5,)),
            pltpu.VMEM((ROWS * HEADS, DIM), f32),
            pltpu.VMEM((ROWS * HEADS, DIM), f32),
            pltpu.VMEM((ROWS * HEADS, DIM), f32),
            pltpu.VMEM((HEADS, 2, ROWS, DIM), bf16),
            pltpu.VMEM((HEADS, ROWS, DIM), bf16),
            pltpu.VMEM((PEERS, 2, ROWS, DIM), bf16),
            pltpu.VMEM((PEERS, ROWS, DIM), bf16),
            pltpu.VMEM((PAIRS, GROUP, SPAN, CHUNK), bf16),
            pltpu.VMEM((PAIRS, GROUP, SPAN, 1), f32),
            pltpu.VMEM((CHUNKS, GROUP, SPAN, 1), f32),
            pltpu.VMEM((CHUNKS, GROUP, SPAN, 1), f32),
            pltpu.VMEM((CHUNKS, GROUP, SPAN, BLOCK), f32),
            pltpu.VMEM((CHUNKS, GROUP, SPAN, DIM), f32),
            pltpu.VMEM((PEERS, ROWS, DIM), bf16),
        ]
        + [dma, dma((CHUNKS,))] * 2 + [dma] * 5 + [pltpu.SemaphoreType.REGULAR],
        compiler_params=pltpu.CompilerParams(
            collective_id=0, has_side_effects=True, vmem_limit_bytes=53 << 20
        ),
    )(*[pltpu.with_memory_space_constraint(operand, pltpu.HBM) for operand in operands])
    return jnp.swapaxes(by_head, 0, 1)


def solution(mesh):
    return jax.shard_map(
        body,
        mesh=mesh,
        in_specs=(
            P(("video", "span", "head"), None, None),
            P(("video", "span", "head"), None, None),
            P(("video", "span", "head"), None, None),
            P("video"),
            P(),
        ),
        out_specs=P(("video", "span", "head"), None, None),
        check_vma=False,
    )
```

```python
import functools
import math

import jax
import jax.numpy as jnp
from jax import lax
from jax.experimental import pallas as pl
from jax.experimental.pallas import tpu as pltpu
from jax.sharding import PartitionSpec as P

MESH = pl.DeviceIdType.MESH
HEADS = 48
DIM = 128
ROWS = 64
SPANS = 16
QUARTERS = 4
SPAN = ROWS * QUARTERS
PEERS = SPANS * QUARTERS
GROUP = 4
CHUNK = SPAN * GROUP
CHUNKS = SPANS // GROUP
BLOCK = 128
HIDDEN = -1e30
SCALE = math.log2(math.e) / math.sqrt(DIM)
PAIRS = CHUNKS * (CHUNKS + 1) // 2


def pair_at(group, chunk):
    return group * (group + 1) // 2 + chunk


def raw_scores(q, keys):
    return lax.dot_general(q, keys, (((1,), (1,)), ((), ())), preferred_element_type=jnp.float32)


def blocks_of(value):
    return [value[:, k * BLOCK : (k + 1) * BLOCK] for k in range(value.shape[1] // BLOCK)]


def fold(parts, op):
    parts = list(parts)
    while len(parts) > 1:
        paired = [op(left, right) for left, right in zip(parts[::2], parts[1::2])]
        parts = paired + (parts[-1:] if len(parts) % 2 else [])
    return parts[0]


def kernel(
    queries_hbm, key_rows_hbm, value_rows_hbm, noise_levels_hbm, gate_table_hbm, got_o,
    queries, key_rows, value_rows, noise_levels, gate_table, loaded, wide_q, wide_k, wide_v, send_qk, send_v, got_qk, got_v, weights, peaks, tops, shares, sums, acc, send_o,
    qk_sent, qk_here, v_sent, v_here, o_sent, o_here, own_qk, own_v, own_o, plane_in,
):
    core = lax.axis_index("video") % 2
    span = lax.axis_index("span")
    x = lax.axis_index("head")
    y = span // 4
    z = span % 4
    me = span * QUARTERS + x

    def place(column_x, column_y, j):
        z_at = (j * 3) // 2 + jnp.where(j == 1, core, 0)
        return (column_y * 4 + column_x) * 3 + j, column_y * 4 + z_at, column_x

    j_far = jnp.where(z < 2, 2, 0)
    j_near = jnp.where(z == 0, 0, jnp.where(z == 3, 2, 1))

    def by_distance(turn):
        return jnp.where(turn == 0, j_far, jnp.where(turn == 2, j_near, 3 - j_far - j_near))

    active = (z == 0) | (z == 3) | (z == 1 + core)
    j_mine = jnp.where(z == 0, 0, jnp.where(z == 3, 2, 1))
    my_head = (y * 4 + x) * 3 + j_mine

    loads = [
        pltpu.make_async_copy(source, target, loaded.at[n])
        for n, (source, target) in enumerate(
            [
                (queries_hbm, queries),
                (key_rows_hbm, key_rows),
                (value_rows_hbm, value_rows),
                (noise_levels_hbm, noise_levels),
                (gate_table_hbm, gate_table),
            ]
        )
    ]
    for load in loads:
        load.start()

    barrier = pltpu.get_barrier_semaphore()

    def signal(semaphore, to_span, to_x):
        pl.semaphore_signal(
            semaphore,
            inc=1,
            device_id={"span": to_span, "head": to_x},
            device_id_type=MESH,
        )

    def greet_column(semaphore):
        for i in range(1, 4):
            signal(semaphore, y * 4 + lax.rem(z + i, 4), x)

    greet_column(barrier)
    for i in range(1, 16):
        signal(barrier, lax.rem(y + i // 4, 4) * 4 + z, lax.rem(x + i % 4, 4))

    def widen(ref, wide):
        wide[...] = ref[...].reshape(ROWS * HEADS, DIM).astype(jnp.float32)

    def head_of(wide, head):
        return wide[pl.ds(head, ROWS, stride=HEADS), :].astype(jnp.bfloat16)

    def lay_out_qk(head):
        send_qk[head, 0] = head_of(wide_q, head)
        send_qk[head, 1] = head_of(wide_k, head)

    def lay_out_v(head):
        send_v[head] = head_of(wide_v, head)

    loads[0].wait()
    widen(queries, wide_q)
    loads[1].wait()
    widen(key_rows, wide_k)
    pl.semaphore_wait(barrier, 3 + 15)
    greet_column(plane_in)

    def send_one(k, turn, stride_y, lay_out, source, target, sent, here, own):
        k_x = k % 4
        k_x = k_x + jnp.where(k_x == 2, 1, 0) - jnp.where(k_x == 3, 1, 0)
        column_x = lax.rem(x + k_x, 4)
        column_y = lax.rem(y + stride_y * (k // 4), 4)
        head, to_span, to_x = place(column_x, column_y, by_distance(turn))
        lay_out(head)
        mine = (to_span == span) & (to_x == x)

        @pl.when(jnp.logical_not(mine))
        def _():
            pltpu.make_async_remote_copy(
                source.at[head],
                target.at[me],
                sent,
                here,
                device_id={"span": to_span, "head": to_x},
                device_id_type=MESH,
            ).start()

        @pl.when(mine)
        def _():
            pltpu.make_async_copy(source.at[head], target.at[me], own).start()

    def scatter_column(*way):
        def one(turn, carry):
            send_one(0, turn, *way)
            return carry

        lax.fori_loop(0, 3, one, 0)

    def scatter_rest(order, *way):
        def one(n, carry):
            k, turn = order(n)

            @pl.when(k > 0)
            def _():
                send_one(k, turn, *way)

            return carry

        lax.fori_loop(0, HEADS, one, 0)

    way_qk = (3, lay_out_qk, send_qk, got_qk, qk_sent, qk_here.at[y], own_qk)
    way_v = (1, lay_out_v, send_v, got_v, v_sent, v_here.at[y], own_v)

    def wait_for(ref, count, semaphore):
        part = ref.at[pl.ds(0, count)]
        pltpu.make_async_copy(part, part, semaphore).wait()

    scatter_column(*way_qk)
    for load in loads[2:]:
        load.wait()
    widen(value_rows, wide_v)
    scatter_column(*way_v)
    pl.semaphore_wait(plane_in, 3)
    def rows_near(n):
        return (n // 12) * 4 + n % 4, 2 - (n % 12) // 4

    def rows_v(n):
        return n % 16, 2 - n // 16

    scatter_rest(rows_near, *way_qk)
    scatter_rest(rows_v, *way_v)

    @pl.when(active)
    def _():
        def q_of(group, r):
            return got_qk[pl.ds((group * GROUP + r) * QUARTERS, QUARTERS), 0].reshape(SPAN, DIM)

        def keys_of(chunk, spans):
            first = chunk * (GROUP * QUARTERS)
            return got_qk[pl.ds(first, spans * QUARTERS), 1].reshape(spans * SPAN, DIM)

        def values_of(chunk, spans):
            first = chunk * (GROUP * QUARTERS)
            return got_v[pl.ds(first, spans * QUARTERS)].reshape(spans * SPAN, DIM)

        def weigh(pair, r, columns, top):
            ws = [jnp.exp2((s - top) * SCALE) for s in columns]
            for k, w in enumerate(ws):
                weights[pair, r, :, k * BLOCK : (k + 1) * BLOCK] = w.astype(jnp.bfloat16)
            peaks[pair, r] = top
            return fold(ws, jnp.add)

        def own_chunk(group):
            for r in range(GROUP):
                columns = blocks_of(raw_scores(q_of(group, r), keys_of(group, r + 1)))
                hidden = jnp.full((BLOCK, BLOCK), HIDDEN, jnp.float32)
                columns[-1] = jnp.concatenate([hidden, columns[-1][BLOCK:]], axis=0)
                top = jnp.max(fold(columns, jnp.maximum), axis=1, keepdims=True)
                sums[group, r] = weigh(pair_at(group, group), r, columns, top)
                tops[group, r] = top

        def earlier_chunk(group, chunk):
            for r in range(GROUP):
                columns = blocks_of(raw_scores(q_of(group, r), keys_of(chunk, GROUP)))
                before = tops[group, r]
                top = jnp.max(fold(columns, jnp.maximum), axis=1, keepdims=True)
                top = jnp.maximum(before, top)
                added = weigh(pair_at(group, chunk), r, columns, top)
                sums[group, r] = sums[group, r] * jnp.exp2((before - top) * SCALE) + added
                tops[group, r] = top

        def row_of(step):
            return lax.rem(y + step, CHUNKS)

        def soften(step, carry):
            row = row_of(step)

            @pl.when(step == 0)
            def _():
                wait_for(got_qk, 15, qk_here.at[row])
                wait_for(got_qk, 1, own_qk)

            @pl.when(step > 0)
            def _():
                wait_for(got_qk, 16, qk_here.at[row])

            own_chunk(row)

            def with_row(before, carry):
                other = row_of(before)
                earlier_chunk(jnp.maximum(row, other), jnp.minimum(row, other))
                return carry

            lax.fori_loop(0, step, with_row, 0)
            return carry

        lax.fori_loop(0, CHUNKS, soften, 0)

        def share(group, carry):
            for r in range(GROUP):
                gate = gate_table[noise_levels[group * GROUP + r], my_head]
                shares[group, r] = gate / jnp.sum(sums[group, r], axis=1, keepdims=True)
                acc[group, r] = jnp.zeros((SPAN, DIM), jnp.float32)
            return carry

        lax.fori_loop(0, CHUNKS, share, 0)

        def add_term(group, chunk, spans, r):
            pair = pair_at(group, chunk)
            rescale = jnp.exp2((peaks[pair, r] - tops[group, r]) * SCALE)
            acc[group, r] += rescale * jnp.dot(
                weights[pair, r, :, 0 : spans * SPAN],
                values_of(chunk, spans),
                preferred_element_type=jnp.float32,
            )

        def give_back(group):
            for r in range(GROUP):
                i = group * GROUP + r
                result = (acc[group, r] * shares[group, r]).astype(jnp.bfloat16)
                send_o[pl.ds(i * QUARTERS, QUARTERS)] = result.reshape(QUARTERS, ROWS, DIM)
                for quarter in range(QUARTERS):
                    piece = i * QUARTERS + quarter
                    mine = piece == me

                    @pl.when(jnp.logical_not(mine))
                    def _():
                        pltpu.make_async_remote_copy(
                            send_o.at[piece],
                            got_o.at[my_head],
                            o_sent,
                            o_here,
                            device_id={"span": i, "head": quarter},
                            device_id_type=MESH,
                        ).start()

                    @pl.when(mine)
                    def _():
                        pltpu.make_async_copy(send_o.at[piece], got_o.at[my_head], own_o).start()

        def gather(step, carry):
            row = lax.rem(y + CHUNKS - step, CHUNKS)

            @pl.when(step == 0)
            def _():
                wait_for(got_v, 15, v_here.at[row])
                wait_for(got_v, 1, own_v)

            @pl.when(step > 0)
            def _():
                wait_for(got_v, 16, v_here.at[row])

            def into(group, carry):
                @pl.when(group == row)
                def _():
                    for r in range(GROUP):
                        add_term(group, group, r + 1, r)

                @pl.when(group > row)
                def _():
                    for r in range(GROUP):
                        add_term(group, row, GROUP, r)

                @pl.when(step == jnp.where(group <= y, y, CHUNKS - 1))
                def _():
                    give_back(group)

                return carry

            lax.fori_loop(row, CHUNKS, into, 0)
            return carry

        lax.fori_loop(0, CHUNKS, gather, 0)
        wait_for(got_o, HEADS - 1, o_here)
        wait_for(got_o, 1, own_o)
        wait_for(send_qk, HEADS - 1, qk_sent)
        wait_for(send_v, HEADS - 1, v_sent)
        wait_for(send_o, PEERS - 1, o_sent)

    @pl.when(jnp.logical_not(active))
    def _():
        wait_for(got_o, HEADS, o_here)
        wait_for(send_qk, HEADS, qk_sent)
        wait_for(send_v, HEADS, v_sent)


def body(*operands):
    hbm = pl.BlockSpec(memory_space=pltpu.HBM)
    anywhere = pl.BlockSpec(memory_space=pl.ANY)
    dma = pltpu.SemaphoreType.DMA
    bf16, f32 = jnp.bfloat16, jnp.float32
    by_head = pl.pallas_call(
        kernel,
        out_shape=jax.ShapeDtypeStruct((HEADS, ROWS, DIM), bf16),
        in_specs=[hbm] * 5,
        out_specs=anywhere,
        scratch_shapes=[pltpu.VMEM((ROWS, HEADS, DIM), bf16)] * 3
        + [
            pltpu.SMEM((SPANS,), jnp.int32),
            pltpu.SMEM((8, HEADS), f32),
            dma((5,)),
            pltpu.VMEM((ROWS * HEADS, DIM), f32),
            pltpu.VMEM((ROWS * HEADS, DIM), f32),
            pltpu.VMEM((ROWS * HEADS, DIM), f32),
            pltpu.VMEM((HEADS, 2, ROWS, DIM), bf16),
            pltpu.VMEM((HEADS, ROWS, DIM), bf16),
            pltpu.VMEM((PEERS, 2, ROWS, DIM), bf16),
            pltpu.VMEM((PEERS, ROWS, DIM), bf16),
            pltpu.VMEM((PAIRS, GROUP, SPAN, CHUNK), bf16),
            pltpu.VMEM((PAIRS, GROUP, SPAN, 1), f32),
            pltpu.VMEM((CHUNKS, GROUP, SPAN, 1), f32),
            pltpu.VMEM((CHUNKS, GROUP, SPAN, 1), f32),
            pltpu.VMEM((CHUNKS, GROUP, SPAN, BLOCK), f32),
            pltpu.VMEM((CHUNKS, GROUP, SPAN, DIM), f32),
            pltpu.VMEM((PEERS, ROWS, DIM), bf16),
        ]
        + [dma, dma((CHUNKS,))] * 2 + [dma] * 5 + [pltpu.SemaphoreType.REGULAR],
        compiler_params=pltpu.CompilerParams(
            collective_id=0, has_side_effects=True, vmem_limit_bytes=53 << 20
        ),
    )(*[pltpu.with_memory_space_constraint(operand, pltpu.HBM) for operand in operands])
    return jnp.swapaxes(by_head, 0, 1)


def solution(mesh):
    return jax.shard_map(
        body,
        mesh=mesh,
        in_specs=(
            P(("video", "span", "head"), None, None),
            P(("video", "span", "head"), None, None),
            P(("video", "span", "head"), None, None),
            P("video"),
            P(),
        ),
        out_specs=P(("video", "span", "head"), None, None),
        check_vma=False,
    )
```
